32 devices in a mesh: harm: 8 (over y, x, core), mode: 4 (over z).
Axes of the slice: x: 2, y: 2, z: 4, core: 2. Of those that a mesh axis runs over, the one named last changes fastest.
Arguments:
- mode_vectors: float32 [49152, 1024], P('harm', 'mode'), may hold values from -0.09375 to 0.09375
- weights: float32 [49152, 1024], P('harm', 'mode'), may hold values from -0.1875 to 0.1875
- cotangent: float32 [49152, 1024], P('harm', 'mode'), may hold values from -6 to 6
- eigenvalues: float32 [1024], replicated, may hold values from 0 to 4
- eigen_cotangent: float32 [1024], replicated, may hold values from -6 to 6
- slab_rows: int32 [4096], replicated, may hold values from 0 to 49151, as said below
Outputs:
- slab: float32 [4096, 49152], P('mode', 'harm')
The draws below stay inside these ranges and needn't reach their ends.
Inputs may be any that keep to these rules, and one draw needn't show every extreme that they name: `slab_rows`: each block of 6144 consecutive harmonics (0 to 6143, 6144 to 12287 and so on) holds exactly 512 of the slab rows.
All inputs are finite; a program needn't handle non-finite values.
Results may differ from the reference program's by a relative error of at most 0.0001.
Values sent between devices are 32-bit elements; how exact they have to be, the bound alone decides.
A program may use at most 128 MiB of HBM per device.

```python
import jax
import jax.numpy as jnp
from jax import lax

H = 49152
K = 1024
R = 4096
HB = 6144
RB = 512


def draw_slab_rows(key, part):
    first_key = jax.random.fold_in(key, 11)
    second_key = jax.random.fold_in(key, 23)
    block_ids = jnp.arange(R, dtype=jnp.int32) // RB
    within = jax.random.randint(first_key, (R,), 0, HB, dtype=jnp.int32)
    values = block_ids * HB + within
    order = jax.random.permutation(second_key, R)
    return jnp.take(values, order, axis=0).astype(jnp.int32)


def levels(key, extent, cuts, low, top_value):
    def one(dim, parts):
        draws = jax.random.uniform(jax.random.fold_in(jax.random.fold_in(key, 6), dim), (parts,), jnp.float32, low / len(cuts), top_value / len(cuts))
        return jnp.repeat(jnp.exp(draws), extent[dim] // parts).reshape((-1,) + (1,) * (len(extent) - dim - 1))

    gain = one(*cuts[0])
    for cut in cuts[1:]:
        gain = gain * one(*cut)
    return gain


def bell_draw(own_key, dims, scale, most, cuts=(), kind=jnp.bfloat16):
    loudness = levels(own_key, dims, cuts, -0.22, 0.18) if cuts else 1.0
    result = jax.random.normal(own_key, dims, jnp.float32) * scale * loudness
    return jnp.minimum(jnp.maximum(result, -most), most).astype(kind)


def setup_inputs(seed: int = 0) -> dict:
    seeds = jax.random.split(jax.random.key(seed), 7)
    return {
        "mode_vectors": bell_draw(seeds[0], (H, K), (4 * K) ** -0.5, 0.09375, ((0, 8), (1, 4)), jnp.float32),
        "weights": bell_draw(seeds[1], (H, K), K ** -0.5, 0.1875, ((0, 8), (1, 4)), jnp.float32),
        "cotangent": bell_draw(seeds[2], (H, K), 1.0, 6.0, ((0, 8), (1, 4)), jnp.float32),
        "eigenvalues": jnp.clip(jax.random.uniform(seeds[3], (K,), jnp.float32, 0.0, 4.0), 0.0, 4.0),
        "eigen_cotangent": bell_draw(seeds[4], (K,), 1.0, 6.0, (), jnp.float32),
        "slab_rows": draw_slab_rows(jax.random.fold_in(seeds[6], 71), 0),
    }


regular = 0.01


def reference(mode_vectors, weights, cotangent, eigenvalues, eigen_cotangent, slab_rows):
    highest = lax.Precision.HIGHEST
    gram = jnp.dot(mode_vectors.T, cotangent, precision=highest, preferred_element_type=jnp.float32)
    differ = eigenvalues[None, :] - eigenvalues[:, None]
    factor = differ / (differ * differ + regular)
    weighted = factor * gram + jnp.diag(eigen_cotangent)
    picked = jnp.take(weights, slab_rows.astype(jnp.int32), axis=0)
    z_rows = jnp.dot(picked, weighted, precision=highest, preferred_element_type=jnp.float32)
    return jnp.dot(z_rows, mode_vectors.T, precision=highest, preferred_element_type=jnp.float32)
```

```python
import functools

import jax
import jax.numpy as jnp
from jax import lax
from jax.experimental import pallas as pl
from jax.experimental.pallas import tpu as pltpu
from jax.sharding import PartitionSpec as P


regular = 0.01
chunks = 4
tile = 512


def product(left, right, left_dim, right_dim):
    return lax.dot_general(
        left,
        right,
        (((left_dim,), (right_dim,)), ((), ())),
        precision=lax.Precision.HIGH,
        preferred_element_type=jnp.float32,
    )


def weigh_gap(block, row_ids, col_ids, eigenvalues, eigen_cotangent):
    eigen_rows = lax.dynamic_slice_in_dim(eigenvalues, row_ids, block.shape[0])
    eigen_cols = lax.dynamic_slice_in_dim(eigenvalues, col_ids, block.shape[1])
    slope_cols = lax.dynamic_slice_in_dim(eigen_cotangent, col_ids, block.shape[1])
    differ = eigen_cols[None, :] - eigen_rows[:, None]
    factor = differ / (differ * differ + regular)
    rows = row_ids + lax.broadcasted_iota(jnp.int32, block.shape, 0)
    cols = col_ids + lax.broadcasted_iota(jnp.int32, block.shape, 1)
    return factor * block + jnp.where(rows == cols, slope_cols[None, :], 0.0)


def pick_rows(table, slab_rows, harm_index):
    row_count = table.shape[0]
    offset = slab_rows - harm_index * row_count
    inside = (offset >= 0) & (offset < row_count)
    picked = jnp.take(table, jnp.clip(offset, 0, row_count - 1), axis=0)
    return jnp.where(inside[:, None], picked, 0.0)


def gather_weights(weights, slab_rows, harm_index, harm_count, mode_count):
    width = weights.shape[1]
    picked = pick_rows(weights, slab_rows, harm_index)
    piece = slab_rows.shape[0] // (harm_count * mode_count)
    picked = picked.reshape(mode_count, harm_count, piece, width)
    picked = lax.psum_scatter(picked, "harm", scatter_dimension=1, tiled=True)
    picked = picked.reshape(mode_count, piece, width)
    swapped = lax.all_to_all(picked, "mode", split_axis=0, concat_axis=2, tiled=True)
    return lax.all_gather(swapped.reshape(piece, mode_count * width), "harm", axis=0, tiled=True)


def plain(mode_vectors, weights, cotangent, eigenvalues, eigen_cotangent, slab_rows, harm_count, mode_count):
    harm_index = lax.axis_index("harm")
    width = mode_vectors.shape[1]
    modes = width * mode_count
    full = lax.all_gather(mode_vectors, "mode", axis=1, tiled=True)
    owned_weights = gather_weights(weights, slab_rows, harm_index, harm_count, mode_count)
    gram = product(full, cotangent, 0, 0)
    gram = lax.psum_scatter(gram, "harm", scatter_dimension=0, tiled=True)
    weighted = weigh_gap(
        gram,
        harm_index * (modes // harm_count),
        lax.axis_index("mode") * width,
        eigenvalues,
        eigen_cotangent,
    )
    weighted = lax.all_gather(weighted, "mode", axis=1, tiled=True)
    weighted = lax.all_gather(weighted, "harm", axis=0, tiled=True)
    return product(product(owned_weights, weighted, 1, 0), full, 1, 1)


def shift(value, pairs):
    return lax.ppermute(value, "mode", pairs)


def split_outside(value):
    high = lax.reduce_precision(value, 8, 7)
    return high.astype(jnp.bfloat16), lax.reduce_precision(value - high, 8, 7).astype(jnp.bfloat16)


def split(value):
    high = value.astype(jnp.bfloat16)
    low = (value - high.astype(jnp.float32)).astype(jnp.bfloat16)
    return high, low


def final_kernel(first_row, pieces, z_ref, own, b1, b2, b3, a1, a2, a3, *rest):
    out_ref, x_buf, x3, sems = rest[-4:]
    step = pl.program_id(0)
    steps = pl.num_programs(0)
    layer = lax.axis_index("mode")
    width = own.shape[1]
    rows = x_buf.shape[1]
    below = {1: b1, 2: b2, 3: b3}
    above = {1: a1, 2: a2, 3: a3}

    def fetch(at, slot):
        for piece in range(pieces):
            for here in range(pieces):

                @pl.when(layer == here)
                def _():
                    delta = piece - here
                    begin = at * rows
                    if delta == 0:
                        source = own
                        begin = first_row + begin
                    else:
                        source = above[delta] if delta > 0 else below[-delta]
                    pltpu.make_async_copy(
                        source.at[pl.ds(begin, rows), :],
                        x_buf.at[slot, :, pl.ds(piece * width, width)],
                        sems.at[slot, piece],
                    ).start()

    slot = lax.rem(step, 2)

    @pl.when(step == 0)
    def _():
        fetch(0, 0)

    @pl.when(step + 1 < steps)
    def _():
        fetch(step + 1, 1 - slot)

    for piece in range(pieces):
        pltpu.make_async_copy(
            own.at[pl.ds(0, rows), :],
            x_buf.at[slot, :, pl.ds(piece * width, width)],
            sems.at[slot, piece],
        ).wait()
    depth = x_buf.shape[2]
    high, low = split(x_buf[slot])
    x3[:, :depth] = high
    x3[:, depth : 2 * depth] = high
    x3[:, 2 * depth :] = low
    out_ref[...] = lax.dot_general(
        z_ref[...], x3[...], (((1,), (1,)), ((), ())), preferred_element_type=jnp.float32
    )


def gram_kernel(lefts, rights, plan, *refs):
    sides = refs[: lefts + len(rights)]
    count = len(plan)
    outs = refs[-2 - count : -2]
    seeds = refs[lefts + len(rights) : -2 - count]
    left3, right3 = refs[-2:]
    rows = sides[0].shape[0]
    slots = [sum(rights[:i]) for i in range(len(rights))]

    @pl.when(pl.program_id(0) == 0)
    def _():
        for index, out in enumerate(outs):
            out[...] = seeds[index][...] if seeds else jnp.zeros_like(out)

    for index in range(lefts):
        width = sides[index].shape[1]
        high, low = split(sides[index][...])
        at = pl.ds(index * width, width)
        left3[:rows, at] = high
        left3[rows : 2 * rows, at] = low
        left3[2 * rows :, at] = high
    for index, fresh in enumerate(rights):
        if not fresh:
            continue
        value = sides[lefts + index][...]
        if index + 1 < len(rights) and not rights[index + 1]:
            value = value + sides[lefts + index + 1][...]
        width = value.shape[1]
        high, low = split(value)
        at = pl.ds(slots[index] * width, width)
        right3[:rows, at] = high
        right3[rows : 2 * rows, at] = high
        right3[2 * rows :, at] = low
    for out, (row, col) in zip(outs, plan):
        high, wide = out.shape
        out[...] += lax.dot_general(
            left3[:, row : row + high],
            right3[:, col : col + wide],
            (((0,), (0,)), ((), ())),
            preferred_element_type=jnp.float32,
        )


def gram_chunk(index, height, lefts, rights, fresh, plan, shapes, seeds):
    width = lefts[0].shape[1]
    steps = height // tile
    first = index * steps
    whole = pl.BlockSpec((tile, width), lambda i: (first + i, 0))
    part = pl.BlockSpec((tile, width), lambda i: (i, 0))
    specs = [part if v.shape[0] == height else whole for v in (*lefts, *rights)]
    fixed = [pl.BlockSpec(s, lambda i: (0, 0)) for s in shapes]
    work = sum(s[0] * s[1] for s in shapes)
    operands = [*lefts, *rights]
    if seeds is not None:
        operands += seeds
        specs += fixed
    return pl.pallas_call(
        functools.partial(gram_kernel, len(lefts), fresh, plan),
        grid=(steps,),
        in_specs=specs,
        out_specs=fixed,
        out_shape=[jax.ShapeDtypeStruct(s, jnp.float32) for s in shapes],
        scratch_shapes=[
            pltpu.VMEM((3 * tile, len(lefts) * width), jnp.bfloat16),
            pltpu.VMEM((3 * tile, sum(fresh) * width), jnp.bfloat16),
        ],
        compiler_params=pltpu.CompilerParams(vmem_limit_bytes=32 * 2**20),
        cost_estimate=pl.CostEstimate(
            flops=6 * work * height,
            bytes_accessed=4 * len(operands) * height * width,
            transcendentals=0,
        ),
        name="gram_chunk",
    )(*operands)


def final_chunk(index, z3, own, lists, previous, columns):
    rows = z3.shape[0]
    width = own.shape[1]
    pieces = z3.shape[1] // (3 * width)
    first_row = index * lists[0].shape[0]
    steps = lists[0].shape[0] // tile
    anywhere = pl.BlockSpec(memory_space=pl.ANY)
    operands = [z3, own, *lists]
    specs = [pl.BlockSpec(z3.shape, lambda i: (0, 0), pipeline_mode=pl.Buffered(1))] + [anywhere] * 7
    aliases = {}
    if previous is not None:
        operands.append(previous)
        specs.append(anywhere)
        aliases = {8: 0}
    first_block = first_row // tile
    return pl.pallas_call(
        functools.partial(final_kernel, first_row, pieces),
        grid=(steps,),
        in_specs=specs,
        out_specs=pl.BlockSpec((rows, tile), lambda i: (0, first_block + i)),
        out_shape=jax.ShapeDtypeStruct((rows, columns), jnp.float32),
        scratch_shapes=[
            pltpu.VMEM((2, tile, pieces * width), jnp.float32),
            pltpu.VMEM((tile, 3 * pieces * width), jnp.bfloat16),
            pltpu.SemaphoreType.DMA((2, pieces)),
        ],
        input_output_aliases=aliases,
        compiler_params=pltpu.CompilerParams(vmem_limit_bytes=40 * 2**20),
        cost_estimate=pl.CostEstimate(
            flops=6 * rows * z3.shape[1] // 3 * steps * tile,
            bytes_accessed=4 * steps * tile * (rows + pieces * width),
            transcendentals=0,
        ),
        name="final_chunk",
    )(*operands)


def slab_order(slab_rows, row_count, harm_count, harm_index):
    total = slab_rows.shape[0]
    share = total // harm_count
    owner = slab_rows // row_count
    ids = lax.broadcasted_iota(jnp.int32, (harm_count, total), 0)
    hit = (owner[None, :] == ids).astype(jnp.int32)
    running = jnp.cumsum(hit, axis=1)
    rank = jnp.sum(hit * running, axis=0) - 1
    position = owner * share + rank
    slots = lax.broadcasted_iota(jnp.int32, (share, total), 0)
    mine = (position - harm_index * share)[None, :] == slots
    offsets = jnp.sum(jnp.where(mine, (slab_rows - harm_index * row_count)[None, :], 0), axis=1)
    return position, offsets


def line_body(mode_vectors, weights, cotangent, eigenvalues, eigen_cotangent, slab_rows, harm_count, mode_count):
    harm = lax.axis_index("harm")
    layer = lax.axis_index("mode")
    height, width = mode_vectors.shape
    total = slab_rows.shape[0]
    lower = layer <= 1
    own = jnp.split(mode_vectors, chunks, 0)
    slope = jnp.split(cotangent, chunks, 0)

    def hop(values, pairs):
        results = []
        for value in values:
            results.append(shift(value, pairs))
        return results

    b1 = hop(own, [(0, 1), (1, 2), (2, 3)])
    a1 = hop(own, [(1, 0), (2, 1), (3, 2)])

    position, offsets = slab_order(slab_rows, height, harm_count, harm)
    picked = jnp.take(weights, offsets, axis=0, mode="clip")
    w_b1 = shift(picked, [(0, 1), (1, 2)])
    w_a1 = shift(picked, [(3, 2), (2, 1)])
    w_third = shift(w_b1, [(1, 2)]) + shift(w_a1, [(2, 1)])
    w_all = jnp.concatenate([picked, w_b1, w_a1, w_third], axis=1)
    w_every = lax.all_gather(w_all, "harm", axis=0, tiled=True)
    w_slab = jnp.take(w_every, position, axis=0, mode="clip")

    b2 = hop(b1, [(1, 2), (2, 3)])
    a2 = hop(a1, [(2, 1), (1, 0)])
    edge = hop(slope, [(0, 1), (3, 2)])
    b3 = hop(b2, [(2, 3)])
    a3 = hop(a2, [(1, 0)])

    part = height // chunks
    near = None
    for c in range(chunks):
        near = gram_chunk(
            c, part, [cotangent], [mode_vectors, b1[c], a1[c]], (1, 1, 1),
            ((0, 0),), ((width, 3 * width),), near,
        )
    far_parts = None
    for c in range(chunks):
        side = edge[c]
        if c == 1:
            side, w_slab = lax.optimization_barrier((side, w_slab))
        far_parts = gram_chunk(
            c, part, [cotangent, side], [mode_vectors, b1[c], a1[c], b2[c], a2[c]], (1, 1, 1, 1, 0),
            ((0, 3 * width), (width, 0)), ((width, width), (width, 4 * width)), far_parts,
        )
    top = jnp.concatenate([near[0], far_parts[0]], axis=1)
    gram = jnp.concatenate([top, far_parts[1]], axis=0)
    gram = lax.psum_scatter(gram, "harm", scatter_dimension=0, tiled=True)

    span = 2 * width // harm_count
    half = harm_count // 2
    last = mode_count - 1
    end = jnp.where(lower, 0, last)
    far = jnp.where(lower, last, 0)
    first_col = jnp.where(harm < half, layer * width + harm * span, end * width + (harm - half) * span)
    blocks = [layer, jnp.maximum(layer - 1, 0), jnp.minimum(layer + 1, last), far]
    row_ids = jnp.concatenate([b * width + jnp.arange(width, dtype=jnp.int32) for b in blocks])
    eigen_i = jnp.concatenate([lax.dynamic_slice_in_dim(eigenvalues, b * width, width) for b in blocks])
    eigen_j = lax.dynamic_slice_in_dim(eigenvalues, first_col, span)
    slope_j = lax.dynamic_slice_in_dim(eigen_cotangent, first_col, span)
    col_ids = first_col + jnp.arange(span, dtype=jnp.int32)
    differ = eigen_j[:, None] - eigen_i[None, :]
    factor = differ / (differ * differ + regular)
    weighted = factor * gram + jnp.where(col_ids[:, None] == row_ids[None, :], slope_j[:, None], 0.0)

    zt = product(weighted, w_slab, 1, 1).reshape(span, mode_count, total // mode_count)
    keep = jnp.where(lower, zt[:, :2], zt[:, 2:])
    give = jnp.where(lower, zt[:, 2:], zt[:, :2])
    got = shift(give, [(1, 2), (2, 1)])
    both = jnp.stack([jnp.where(lower, keep, got), jnp.where(lower, got, keep)])
    outer = shift(jnp.where(lower, both[:, :, 0], both[:, :, 1]), [(1, 0), (2, 3)])
    inner = jnp.where(lower, both[:, :, 1], both[:, :, 0])
    mine = jnp.where((layer == 0) | (layer == last), outer, inner)
    every = lax.all_gather(mine, "harm", axis=0, tiled=False)
    zt = jnp.concatenate(
        [every[half:, 0], every[:half, 0], every[:half, 1], every[half:, 1]], axis=0
    ).reshape(mode_count * width, total // mode_count)
    high, low = split_outside(zt.T)
    z3 = jnp.concatenate([high, low, high], axis=1)

    out = None
    for c in range(chunks):
        out = final_chunk(c, z3, mode_vectors, [b1[c], b2[c], b3[c], a1[c], a2[c], a3[c]], out, height)
    return out


def line(*operands):
    return line_body(*operands)


def solution(mesh):
    harm_count = mesh.shape["harm"]
    mode_count = mesh.shape["mode"]
    placed = (P("harm", "mode"), P("harm", "mode"), P("harm", "mode"), P(), P(), P())
    form = line if mode_count == 4 else plain

    def local(*operands):
        return form(*operands, harm_count, mode_count)

    return jax.shard_map(
        local, mesh=mesh, in_specs=placed, out_specs=P("mode", "harm"), check_vma=False
    )
```

```python
import functools

import jax
import jax.numpy as jnp
from jax import lax
from jax.experimental import pallas as pl
from jax.experimental.pallas import tpu as pltpu
from jax.sharding import PartitionSpec as P


regular = 0.01
chunks = 4
tile = 512


def product(left, right, left_dim, right_dim):
    return lax.dot_general(
        left,
        right,
        (((left_dim,), (right_dim,)), ((), ())),
        precision=lax.Precision.HIGH,
        preferred_element_type=jnp.float32,
    )


def weigh_gap(block, row_ids, col_ids, eigenvalues, eigen_cotangent):
    eigen_rows = lax.dynamic_slice_in_dim(eigenvalues, row_ids, block.shape[0])
    eigen_cols = lax.dynamic_slice_in_dim(eigenvalues, col_ids, block.shape[1])
    slope_cols = lax.dynamic_slice_in_dim(eigen_cotangent, col_ids, block.shape[1])
    differ = eigen_cols[None, :] - eigen_rows[:, None]
    factor = differ / (differ * differ + regular)
    rows = row_ids + lax.broadcasted_iota(jnp.int32, block.shape, 0)
    cols = col_ids + lax.broadcasted_iota(jnp.int32, block.shape, 1)
    return factor * block + jnp.where(rows == cols, slope_cols[None, :], 0.0)


def pick_rows(table, slab_rows, harm_index):
    row_count = table.shape[0]
    offset = slab_rows - harm_index * row_count
    inside = (offset >= 0) & (offset < row_count)
    picked = jnp.take(table, jnp.clip(offset, 0, row_count - 1), axis=0)
    return jnp.where(inside[:, None], picked, 0.0)


def gather_weights(weights, slab_rows, harm_index, harm_count, mode_count):
    width = weights.shape[1]
    picked = pick_rows(weights, slab_rows, harm_index)
    piece = slab_rows.shape[0] // (harm_count * mode_count)
    picked = picked.reshape(mode_count, harm_count, piece, width)
    picked = lax.psum_scatter(picked, "harm", scatter_dimension=1, tiled=True)
    picked = picked.reshape(mode_count, piece, width)
    swapped = lax.all_to_all(picked, "mode", split_axis=0, concat_axis=2, tiled=True)
    return lax.all_gather(swapped.reshape(piece, mode_count * width), "harm", axis=0, tiled=True)


def plain(mode_vectors, weights, cotangent, eigenvalues, eigen_cotangent, slab_rows, harm_count, mode_count):
    harm_index = lax.axis_index("harm")
    width = mode_vectors.shape[1]
    modes = width * mode_count
    full = lax.all_gather(mode_vectors, "mode", axis=1, tiled=True)
    owned_weights = gather_weights(weights, slab_rows, harm_index, harm_count, mode_count)
    gram = product(full, cotangent, 0, 0)
    gram = lax.psum_scatter(gram, "harm", scatter_dimension=0, tiled=True)
    weighted = weigh_gap(
        gram,
        harm_index * (modes // harm_count),
        lax.axis_index("mode") * width,
        eigenvalues,
        eigen_cotangent,
    )
    weighted = lax.all_gather(weighted, "mode", axis=1, tiled=True)
    weighted = lax.all_gather(weighted, "harm", axis=0, tiled=True)
    return product(product(owned_weights, weighted, 1, 0), full, 1, 1)


def shift(value, pairs):
    return lax.ppermute(value, "mode", pairs)


def split(value):
    high = value.astype(jnp.bfloat16)
    low = (value - high.astype(jnp.float32)).astype(jnp.bfloat16)
    return high, low


def final_kernel(first_row, pieces, parts, z_ref, own, *rest):
    lists = [rest[6 * c : 6 * c + 6] for c in range(parts)]
    out_ref, x_buf, x3, sems = rest[-4:]
    step = pl.program_id(0)
    steps = pl.num_programs(0)
    each = steps // parts
    layer = lax.axis_index("mode")
    width = own.shape[1]
    rows = x_buf.shape[1]

    def fetch(at, slot, chosen):
        for c in chosen:
            for piece in range(pieces):
                for here in range(pieces):
                    delta = piece - here

                    @pl.when((layer == here) & (at >= c * each) & (at < (c + 1) * each))
                    def _():
                        if delta == 0:
                            source, begin = own, first_row + at * rows
                        else:
                            source = lists[c][2 + delta if delta > 0 else -delta - 1]
                            begin = (at - c * each) * rows
                        pltpu.make_async_copy(
                            source.at[pl.ds(begin, rows), :],
                            x_buf.at[slot, :, pl.ds(piece * width, width)],
                            sems.at[slot, piece],
                        ).start()

    slot = lax.rem(step, 2)

    @pl.when(step == 0)
    def _():
        fetch(step, 0, (0,))

    @pl.when(step + 1 < steps)
    def _():
        fetch(step + 1, 1 - slot, range(parts))

    for piece in range(pieces):
        pltpu.make_async_copy(
            own.at[pl.ds(0, rows), :],
            x_buf.at[slot, :, pl.ds(piece * width, width)],
            sems.at[slot, piece],
        ).wait()
    depth = x_buf.shape[2]
    high, low = split(x_buf[slot])
    x3[:, :depth] = high
    x3[:, depth : 2 * depth] = high
    x3[:, 2 * depth :] = low
    out_ref[...] = lax.dot_general(
        z_ref[...], x3[...], (((1,), (1,)), ((), ())), preferred_element_type=jnp.float32
    )


def gram_kernel(lefts, rights, plan, *refs):
    sides = refs[: lefts + len(rights)]
    count = len(plan)
    outs = refs[-2 - count : -2]
    seeds = refs[lefts + len(rights) : -2 - count]
    left3, right3 = refs[-2:]
    rows = sides[0].shape[0]
    slots = [sum(rights[:i]) for i in range(len(rights))]

    @pl.when(pl.program_id(0) == 0)
    def _():
        for index, out in enumerate(outs):
            out[...] = seeds[index][...] if seeds else jnp.zeros_like(out)

    for index in range(lefts):
        width = sides[index].shape[1]
        high, low = split(sides[index][...])
        at = pl.ds(index * width, width)
        left3[:rows, at] = high
        left3[rows : 2 * rows, at] = low
        left3[2 * rows :, at] = high
    for index, fresh in enumerate(rights):
        if not fresh:
            continue
        value = sides[lefts + index][...]
        if index + 1 < len(rights) and not rights[index + 1]:
            value = value + sides[lefts + index + 1][...]
        width = value.shape[1]
        high, low = split(value)
        at = pl.ds(slots[index] * width, width)
        right3[:rows, at] = high
        right3[rows : 2 * rows, at] = high
        right3[2 * rows :, at] = low
    for out, (row, col) in zip(outs, plan):
        high, wide = out.shape
        out[...] += lax.dot_general(
            left3[:, row : row + high],
            right3[:, col : col + wide],
            (((0,), (0,)), ((), ())),
            preferred_element_type=jnp.float32,
        )


def gram_chunk(index, height, lefts, rights, fresh, plan, shapes, seeds):
    width = lefts[0].shape[1]
    steps = height // tile
    first = index * steps
    whole = pl.BlockSpec((tile, width), lambda i: (first + i, 0))
    part = pl.BlockSpec((tile, width), lambda i: (i, 0))
    specs = [part if v.shape[0] == height else whole for v in (*lefts, *rights)]
    fixed = [pl.BlockSpec(s, lambda i: (0, 0)) for s in shapes]
    work = sum(s[0] * s[1] for s in shapes)
    operands = [*lefts, *rights]
    if seeds is not None:
        operands += seeds
        specs += fixed
    return pl.pallas_call(
        functools.partial(gram_kernel, len(lefts), fresh, plan),
        grid=(steps,),
        in_specs=specs,
        out_specs=fixed,
        out_shape=[jax.ShapeDtypeStruct(s, jnp.float32) for s in shapes],
        scratch_shapes=[
            pltpu.VMEM((3 * tile, len(lefts) * width), jnp.bfloat16),
            pltpu.VMEM((3 * tile, sum(fresh) * width), jnp.bfloat16),
        ],
        compiler_params=pltpu.CompilerParams(vmem_limit_bytes=32 * 2**20),
        cost_estimate=pl.CostEstimate(
            flops=6 * work * height,
            bytes_accessed=4 * len(operands) * height * width,
            transcendentals=0,
        ),
        name="gram_chunk",
    )(*operands)


def final_chunk(index, z3, own, groups, previous, columns):
    rows = z3.shape[0]
    width = own.shape[1]
    pieces = z3.shape[1] // (3 * width)
    lists = [v for group in groups for v in group]
    first_row = index * lists[0].shape[0]
    steps = len(groups) * (lists[0].shape[0] // tile)
    anywhere = pl.BlockSpec(memory_space=pl.ANY)
    operands = [z3, own, *lists]
    specs = [pl.BlockSpec(z3.shape, lambda i: (0, 0), pipeline_mode=pl.Buffered(1))]
    specs += [anywhere] * (1 + len(lists))
    aliases = {}
    if previous is not None:
        aliases = {len(operands): 0}
        operands.append(previous)
        specs.append(anywhere)
    first_block = first_row // tile
    return pl.pallas_call(
        functools.partial(final_kernel, first_row, pieces, len(groups)),
        grid=(steps,),
        in_specs=specs,
        out_specs=pl.BlockSpec((rows, tile), lambda i: (0, first_block + i)),
        out_shape=jax.ShapeDtypeStruct((rows, columns), jnp.float32),
        scratch_shapes=[
            pltpu.VMEM((2, tile, pieces * width), jnp.float32),
            pltpu.VMEM((tile, 3 * pieces * width), jnp.bfloat16),
            pltpu.SemaphoreType.DMA((2, pieces)),
        ],
        input_output_aliases=aliases,
        compiler_params=pltpu.CompilerParams(vmem_limit_bytes=40 * 2**20),
        cost_estimate=pl.CostEstimate(
            flops=2 * rows * z3.shape[1] * steps * tile,
            bytes_accessed=4 * steps * tile * (rows + pieces * width),
            transcendentals=0,
        ),
        name="final_chunk",
    )(*operands)


MESH = pl.DeviceIdType.MESH


def send(source, target, send_sem, recv_sem, device):
    return pltpu.make_async_remote_copy(
        src_ref=source,
        dst_ref=target,
        send_sem=send_sem,
        recv_sem=recv_sem,
        device_id=device,
        device_id_type=MESH,
    )


def greet(device):
    pl.semaphore_signal(pltpu.get_barrier_semaphore(), inc=1, device_id=device, device_id_type=MESH)


def chain_kernel(
    chips, gram, table, eigen_j, eigen_i, ids_j, ids_i, slope_j, mine,
    met, total, came, w_tiles, w_high, w_low, zt, got, land,
    w_sems, met_send, met_recv, came_send, came_recv, z_send, z_recv,
):
    me = lax.axis_index("harm")
    layer = lax.axis_index("mode")
    core = lax.rem(me, 2)
    chip = lax.div(me, 2)
    partner = me + 1 - 2 * core
    middle = (layer == 1) | (layer == 2)
    span = met.shape[1]
    tiles, rows = w_tiles.shape[:2]
    peer = 3 - layer
    end = jnp.where(layer == 1, 0, 3)
    keep = jnp.where(layer == 1, 0, 2)
    slot = jnp.where(layer == 1, 0, 1)

    @pl.when(middle)
    def _():
        greet({"harm": partner})
        for d in range(1, chips):
            greet({"harm": lax.rem(chip + d, chips) * 2 + core})
        greet({"mode": layer - 1})
        greet({"mode": layer + 1})
        pl.semaphore_wait(pltpu.get_barrier_semaphore(), chips + 2)
        first = [
            send(
                gram.at[pl.ds((2 * q + 1 - core) * span, span), :],
                met.at[q],
                met_send.at[q],
                met_recv.at[q],
                {"harm": partner},
            )
            for q in range(chips)
        ]
        for copy in first:
            copy.start()
        loads = [
            pltpu.make_async_copy(table.at[pl.ds(t * rows, rows), :], w_tiles.at[t], w_sems.at[t])
            for t in range(tiles)
        ]
        for load in loads:
            load.start()
        for q in range(chips):
            first[q].wait()
            total[q] = gram[pl.ds((2 * q + core) * span, span), :] + met[q]
        second = []
        for d in range(1, chips):
            q = lax.rem(chip + d, chips)
            second.append(
                send(
                    total.at[q],
                    came.at[d - 1],
                    came_send.at[d - 1],
                    came_recv.at[d - 1],
                    {"harm": q * 2 + core},
                )
            )
            second[-1].start()
        for load in loads:
            load.wait()

        def cut(t, carry):
            high, low = split(w_tiles[t])
            w_high[t] = high
            w_low[t] = low
            return carry

        lax.fori_loop(0, tiles, cut, 0)
        for copy in second:
            copy.wait()
        value = total[chip]
        for d in range(1, chips):
            value = value + came[d - 1]
        differ = eigen_j[...] - eigen_i[...]
        value = value * (differ / (differ * differ + regular))
        value = value + jnp.where(ids_j[...] == ids_i[...], slope_j[...], 0.0)
        high, low = split(value)
        both = jnp.concatenate([high, low], axis=0)
        per = zt.shape[2] // rows
        nt = (((1,), (1,)), ((), ()))

        def mix(t, carry):
            part = lax.dot_general(both, w_high[t], nt, preferred_element_type=jnp.float32)
            rest = lax.dot_general(high, w_low[t], nt, preferred_element_type=jnp.float32)
            zt[t // per, :, pl.ds(pl.multiple_of(lax.rem(t, per) * rows, rows), rows)] = (
                part[:span] + part[span:] + rest
            )
            return carry

        lax.fori_loop(0, tiles, mix, 0)
        swap = send(zt.at[pl.ds(2 - keep, 2)], got, z_send.at[0], z_recv.at[0], {"mode": peer})
        swap.start()
        out = send(zt.at[end], land.at[slot], z_send.at[1], z_recv.at[1], {"mode": end})
        out.start()
        mine[slot] = zt[layer]
        swap.wait()
        pass_on = send(
            got.at[end - keep], land.at[1 - slot], z_send.at[2], z_recv.at[2], {"mode": end}
        )
        pass_on.start()
        mine[1 - slot] = got[layer - keep]
        out.wait_send()
        pass_on.wait_send()

    @pl.when(jnp.logical_not(middle))
    def _():
        inward = jnp.where(layer == 0, 1, 2)
        side = jnp.where(layer == 0, 0, 1)
        greet({"mode": inward})
        pl.semaphore_wait(pltpu.get_barrier_semaphore(), 1)
        send(zt.at[0], land.at[side], z_send.at[1], z_recv.at[1], {"mode": inward}).wait_recv()
        send(zt.at[0], land.at[1 - side], z_send.at[2], z_recv.at[2], {"mode": inward}).wait_recv()
        mine[...] = land[...]


def chain(gram, table, eigen_j, eigen_i, ids_j, ids_i, slope_j, harm_count, mode_count):
    chips = harm_count // 2
    span = gram.shape[0] // harm_count
    modes = gram.shape[1]
    rows = table.shape[0] // mode_count
    cut = 512
    tiles = table.shape[0] // cut
    vmem = pl.BlockSpec(memory_space=pltpu.VMEM)
    return pl.pallas_call(
        functools.partial(chain_kernel, chips),
        in_specs=[vmem, pl.BlockSpec(memory_space=pl.ANY)] + [vmem] * 5,
        out_specs=vmem,
        out_shape=jax.ShapeDtypeStruct((2, span, rows), jnp.float32),
        scratch_shapes=[
            pltpu.VMEM((chips, span, modes), jnp.float32),
            pltpu.VMEM((chips, span, modes), jnp.float32),
            pltpu.VMEM((chips - 1, span, modes), jnp.float32),
            pltpu.VMEM((tiles, cut, modes), jnp.float32),
            pltpu.VMEM((tiles, cut, modes), jnp.bfloat16),
            pltpu.VMEM((tiles, cut, modes), jnp.bfloat16),
            pltpu.VMEM((mode_count, span, rows), jnp.float32),
            pltpu.VMEM((2, span, rows), jnp.float32),
            pltpu.VMEM((2, span, rows), jnp.float32),
            pltpu.SemaphoreType.DMA((tiles,)),
            pltpu.SemaphoreType.DMA((chips,)),
            pltpu.SemaphoreType.DMA((chips,)),
            pltpu.SemaphoreType.DMA((chips - 1,)),
            pltpu.SemaphoreType.DMA((chips - 1,)),
            pltpu.SemaphoreType.DMA((3,)),
            pltpu.SemaphoreType.DMA((3,)),
        ],
        compiler_params=pltpu.CompilerParams(
            collective_id=1, has_side_effects=True, vmem_limit_bytes=52 * 2**20
        ),
        name="chain",
    )(gram, table, eigen_j, eigen_i, ids_j, ids_i, slope_j)


def spread_kernel(chips, width, mine, z_ref, land, out_send, out_recv, pair_send, pair_recv):
    me = lax.axis_index("harm")
    core = lax.rem(me, 2)
    chip = lax.div(me, 2)
    partner = me + 1 - 2 * core
    greet({"harm": partner})
    for d in range(1, chips):
        greet({"harm": lax.rem(chip + d, chips) * 2 + core})
    pl.semaphore_wait(pltpu.get_barrier_semaphore(), chips)
    outward = []
    for d in range(1, chips):
        outward.append(
            send(
                mine,
                land.at[chip, core],
                out_send.at[d - 1],
                out_recv.at[d - 1],
                {"harm": lax.rem(chip + d, chips) * 2 + core},
            )
        )
        outward[-1].start()
    paired = [send(mine, land.at[chip, core], pair_send.at[0], pair_recv.at[0], {"harm": partner})]
    paired[0].start()
    land[chip, core] = mine[...]
    for d in range(1, chips):
        origin = lax.rem(chip + chips - d, chips)
        outward[d - 1].wait()
        paired.append(
            send(
                land.at[origin, core],
                land.at[origin, core],
                pair_send.at[d],
                pair_recv.at[d],
                {"harm": partner},
            )
        )
        paired[-1].start()
    for copy in paired:
        copy.wait()
    depth = z_ref.shape[1] // 3
    half = chips // 2
    for q in range(chips):
        for side in range(2):
            piece = 1 - q // half if side == 0 else 2 + q // half
            block = jnp.concatenate([land[q, 0, side], land[q, 1, side]], axis=0).T
            high, low = split(block)
            at = piece * width + (q % half) * block.shape[1]
            size = block.shape[1]
            z_ref[:, at : at + size] = high
            z_ref[:, depth + at : depth + at + size] = low
            z_ref[:, 2 * depth + at : 2 * depth + at + size] = high


def spread(mine, harm_count, mode_count, width):
    chips = harm_count // 2
    vmem = pl.BlockSpec(memory_space=pltpu.VMEM)
    return pl.pallas_call(
        functools.partial(spread_kernel, chips, width),
        in_specs=[vmem],
        out_specs=vmem,
        out_shape=jax.ShapeDtypeStruct((mine.shape[2], 3 * mode_count * width), jnp.bfloat16),
        scratch_shapes=[
            pltpu.VMEM((chips, 2, *mine.shape), jnp.float32),
            pltpu.SemaphoreType.DMA((chips - 1,)),
            pltpu.SemaphoreType.DMA((chips - 1,)),
            pltpu.SemaphoreType.DMA((chips,)),
            pltpu.SemaphoreType.DMA((chips,)),
        ],
        compiler_params=pltpu.CompilerParams(
            collective_id=2, has_side_effects=True, vmem_limit_bytes=40 * 2**20
        ),
        name="spread",
    )(mine)


def slab_order(slab_rows, row_count, harm_count, harm_index):
    total = slab_rows.shape[0]
    share = total // harm_count
    owner = slab_rows // row_count
    ids = lax.broadcasted_iota(jnp.int32, (harm_count, total), 0)
    hit = (owner[None, :] == ids).astype(jnp.int32)
    running = jnp.cumsum(hit, axis=1)
    rank = jnp.sum(hit * running, axis=0) - 1
    position = owner * share + rank
    slots = lax.broadcasted_iota(jnp.int32, (share, total), 0)
    mine = (position - harm_index * share)[None, :] == slots
    offsets = jnp.sum(jnp.where(mine, (slab_rows - harm_index * row_count)[None, :], 0), axis=1)
    return position, offsets


def line_body(mode_vectors, weights, cotangent, eigenvalues, eigen_cotangent, slab_rows, harm_count, mode_count):
    harm = lax.axis_index("harm")
    layer = lax.axis_index("mode")
    height, width = mode_vectors.shape
    lower = layer <= 1
    own = jnp.split(mode_vectors, chunks, 0)
    slope = jnp.split(cotangent, chunks, 0)

    def hop(values, pairs):
        results = []
        for value in values:
            results.append(shift(value, pairs))
        return results

    b1 = hop(own, [(0, 1), (1, 2), (2, 3)])
    a1 = hop(own, [(1, 0), (2, 1), (3, 2)])

    position, offsets = slab_order(slab_rows, height, harm_count, harm)
    picked = jnp.take(weights, offsets, axis=0, mode="clip")
    w_b1 = shift(picked, [(0, 1), (1, 2)])
    w_a1 = shift(picked, [(3, 2), (2, 1)])
    w_third = shift(w_b1, [(1, 2)]) + shift(w_a1, [(2, 1)])
    w_all = jnp.concatenate([picked, w_b1, w_a1, w_third], axis=1)
    w_every = lax.all_gather(w_all, "harm", axis=0, tiled=True)
    w_slab = jnp.take(w_every, position, axis=0, mode="clip")

    b2 = hop(b1, [(1, 2), (2, 3)])
    a2 = hop(a1, [(2, 1), (1, 0)])
    edge = hop(slope, [(0, 1), (3, 2)])
    b3 = hop(b2, [(2, 3)])
    a3 = hop(a2, [(1, 0)])

    part = height // chunks
    near = None
    for c in range(chunks):
        near = gram_chunk(
            c, part, [cotangent], [mode_vectors, b1[c], a1[c]], (1, 1, 1),
            ((0, 0),), ((width, 3 * width),), near,
        )
    far_parts = None
    for c in range(chunks):
        side = edge[c]
        if c == 1:
            side, w_slab = lax.optimization_barrier((side, w_slab))
        far_parts = gram_chunk(
            c, part, [cotangent, side], [mode_vectors, b1[c], a1[c], b2[c], a2[c]], (1, 1, 1, 1, 0),
            ((0, 3 * width), (width, 0)), ((width, width), (width, 4 * width)), far_parts,
        )
    top = jnp.concatenate([near[0], far_parts[0]], axis=1)
    gram = jnp.concatenate([top, far_parts[1]], axis=0)

    span = 2 * width // harm_count
    half = harm_count // 2
    last = mode_count - 1
    end = jnp.where(lower, 0, last)
    far = jnp.where(lower, last, 0)
    first_col = jnp.where(harm < half, layer * width + harm * span, end * width + (harm - half) * span)
    blocks = [layer, jnp.maximum(layer - 1, 0), jnp.minimum(layer + 1, last), far]
    row_ids = jnp.concatenate([b * width + jnp.arange(width, dtype=jnp.int32) for b in blocks])
    eigen_i = jnp.concatenate([lax.dynamic_slice_in_dim(eigenvalues, b * width, width) for b in blocks])
    eigen_j = lax.dynamic_slice_in_dim(eigenvalues, first_col, span)
    slope_j = lax.dynamic_slice_in_dim(eigen_cotangent, first_col, span)
    col_ids = first_col + jnp.arange(span, dtype=jnp.int32)
    mine = chain(
        gram, w_slab, eigen_j[:, None], eigen_i[None, :], col_ids[:, None], row_ids[None, :],
        slope_j[:, None], harm_count, mode_count,
    )
    z3 = spread(mine, harm_count, mode_count, width)

    out = None
    lists = list(zip(b1, b2, b3, a1, a2, a3))
    for first, count in ((0, 2), (2, 1), (3, 1)):
        out = final_chunk(first, z3, mode_vectors, lists[first : first + count], out, height)
    return out


def line(*operands):
    return line_body(*operands)


def solution(mesh):
    harm_count = mesh.shape["harm"]
    mode_count = mesh.shape["mode"]
    placed = (P("harm", "mode"), P("harm", "mode"), P("harm", "mode"), P(), P(), P())
    form = line if mode_count == 4 else plain

    def local(*operands):
        return form(*operands, harm_count, mode_count)

    return jax.shard_map(
        local, mesh=mesh, in_specs=placed, out_specs=P("mode", "harm"), check_vma=False
    )
```

```python
import functools

import jax
import jax.numpy as jnp
from jax import lax
from jax.experimental import pallas as pl
from jax.experimental.pallas import tpu as pltpu
from jax.sharding import PartitionSpec as P


regular = 0.01
chunks = 4
tile = 512


def product(left, right, left_dim, right_dim):
    return lax.dot_general(
        left,
        right,
        (((left_dim,), (right_dim,)), ((), ())),
        precision=lax.Precision.HIGH,
        preferred_element_type=jnp.float32,
    )


def weigh_gap(block, row_ids, col_ids, eigenvalues, eigen_cotangent):
    eigen_rows = lax.dynamic_slice_in_dim(eigenvalues, row_ids, block.shape[0])
    eigen_cols = lax.dynamic_slice_in_dim(eigenvalues, col_ids, block.shape[1])
    slope_cols = lax.dynamic_slice_in_dim(eigen_cotangent, col_ids, block.shape[1])
    differ = eigen_cols[None, :] - eigen_rows[:, None]
    factor = differ / (differ * differ + regular)
    rows = row_ids + lax.broadcasted_iota(jnp.int32, block.shape, 0)
    cols = col_ids + lax.broadcasted_iota(jnp.int32, block.shape, 1)
    return factor * block + jnp.where(rows == cols, slope_cols[None, :], 0.0)


def pick_rows(table, slab_rows, harm_index):
    row_count = table.shape[0]
    offset = slab_rows - harm_index * row_count
    inside = (offset >= 0) & (offset < row_count)
    picked = jnp.take(table, jnp.clip(offset, 0, row_count - 1), axis=0)
    return jnp.where(inside[:, None], picked, 0.0)


def gather_weights(weights, slab_rows, harm_index, harm_count, mode_count):
    width = weights.shape[1]
    picked = pick_rows(weights, slab_rows, harm_index)
    piece = slab_rows.shape[0] // (harm_count * mode_count)
    picked = picked.reshape(mode_count, harm_count, piece, width)
    picked = lax.psum_scatter(picked, "harm", scatter_dimension=1, tiled=True)
    picked = picked.reshape(mode_count, piece, width)
    swapped = lax.all_to_all(picked, "mode", split_axis=0, concat_axis=2, tiled=True)
    return lax.all_gather(swapped.reshape(piece, mode_count * width), "harm", axis=0, tiled=True)


def plain(mode_vectors, weights, cotangent, eigenvalues, eigen_cotangent, slab_rows, harm_count, mode_count):
    harm_index = lax.axis_index("harm")
    width = mode_vectors.shape[1]
    modes = width * mode_count
    full = lax.all_gather(mode_vectors, "mode", axis=1, tiled=True)
    owned_weights = gather_weights(weights, slab_rows, harm_index, harm_count, mode_count)
    gram = product(full, cotangent, 0, 0)
    gram = lax.psum_scatter(gram, "harm", scatter_dimension=0, tiled=True)
    weighted = weigh_gap(
        gram,
        harm_index * (modes // harm_count),
        lax.axis_index("mode") * width,
        eigenvalues,
        eigen_cotangent,
    )
    weighted = lax.all_gather(weighted, "mode", axis=1, tiled=True)
    weighted = lax.all_gather(weighted, "harm", axis=0, tiled=True)
    return product(product(owned_weights, weighted, 1, 0), full, 1, 1)


def shift(value, pairs):
    return lax.ppermute(value, "mode", pairs)


def split(value):
    high = value.astype(jnp.bfloat16)
    low = (value - high.astype(jnp.float32)).astype(jnp.bfloat16)
    return high, low


def final_kernel(first_row, pieces, parts, z_ref, own, *rest):
    lists = [rest[6 * c : 6 * c + 6] for c in range(parts)]
    out_ref, x_buf, x3, sems = rest[-4:]
    step = pl.program_id(0)
    steps = pl.num_programs(0)
    each = steps // parts
    layer = lax.axis_index("mode")
    width = own.shape[1]
    rows = x_buf.shape[1]

    def fetch(at, slot, chosen):
        for c in chosen:
            for piece in range(pieces):
                for here in range(pieces):
                    delta = piece - here

                    @pl.when((layer == here) & (at >= c * each) & (at < (c + 1) * each))
                    def _():
                        if delta == 0:
                            source, begin = own, first_row + at * rows
                        else:
                            source = lists[c][2 + delta if delta > 0 else -delta - 1]
                            begin = (at - c * each) * rows
                        pltpu.make_async_copy(
                            source.at[pl.ds(begin, rows), :],
                            x_buf.at[slot, :, pl.ds(piece * width, width)],
                            sems.at[slot, piece],
                        ).start()

    slot = lax.rem(step, 2)

    @pl.when(step == 0)
    def _():
        fetch(step, 0, (0,))

    @pl.when(step + 1 < steps)
    def _():
        fetch(step + 1, 1 - slot, range(parts))

    for piece in range(pieces):
        pltpu.make_async_copy(
            own.at[pl.ds(0, rows), :],
            x_buf.at[slot, :, pl.ds(piece * width, width)],
            sems.at[slot, piece],
        ).wait()
    depth = x_buf.shape[2]
    high, low = split(x_buf[slot])
    x3[:, :depth] = high
    x3[:, depth : 2 * depth] = high
    x3[:, 2 * depth :] = low
    out_ref[...] = lax.dot_general(
        z_ref[...], x3[...], (((1,), (1,)), ((), ())), preferred_element_type=jnp.float32
    )


def gram_kernel(lefts, rights, plan, *refs):
    sides = refs[: lefts + len(rights)]
    count = len(plan)
    outs = refs[-2 - count : -2]
    seeds = refs[lefts + len(rights) : -2 - count]
    left3, right3 = refs[-2:]
    rows = sides[0].shape[0]
    slots = [sum(rights[:i]) for i in range(len(rights))]

    @pl.when(pl.program_id(0) == 0)
    def _():
        for index, out in enumerate(outs):
            out[...] = seeds[index][...] if seeds else jnp.zeros_like(out)

    for index in range(lefts):
        width = sides[index].shape[1]
        high, low = split(sides[index][...])
        at = pl.ds(index * width, width)
        left3[:rows, at] = high
        left3[rows : 2 * rows, at] = low
        left3[2 * rows :, at] = high
    for index, fresh in enumerate(rights):
        if not fresh:
            continue
        value = sides[lefts + index][...]
        if index + 1 < len(rights) and not rights[index + 1]:
            value = value + sides[lefts + index + 1][...]
        width = value.shape[1]
        high, low = split(value)
        at = pl.ds(slots[index] * width, width)
        right3[:rows, at] = high
        right3[rows : 2 * rows, at] = high
        right3[2 * rows :, at] = low
    for out, (row, col) in zip(outs, plan):
        high, wide = out.shape
        out[...] += lax.dot_general(
            left3[:, row : row + high],
            right3[:, col : col + wide],
            (((0,), (0,)), ((), ())),
            preferred_element_type=jnp.float32,
        )


def gram_chunk(index, height, lefts, rights, fresh, plan, shapes, seeds):
    width = lefts[0].shape[1]
    steps = height // tile
    first = index * steps
    whole = pl.BlockSpec((tile, width), lambda i: (first + i, 0))
    part = pl.BlockSpec((tile, width), lambda i: (i, 0))
    specs = [part if v.shape[0] == height else whole for v in (*lefts, *rights)]
    fixed = [pl.BlockSpec(s, lambda i: (0, 0)) for s in shapes]
    work = sum(s[0] * s[1] for s in shapes)
    operands = [*lefts, *rights]
    if seeds is not None:
        operands += seeds
        specs += fixed
    return pl.pallas_call(
        functools.partial(gram_kernel, len(lefts), fresh, plan),
        grid=(steps,),
        in_specs=specs,
        out_specs=fixed,
        out_shape=[jax.ShapeDtypeStruct(s, jnp.float32) for s in shapes],
        scratch_shapes=[
            pltpu.VMEM((3 * tile, len(lefts) * width), jnp.bfloat16),
            pltpu.VMEM((3 * tile, sum(fresh) * width), jnp.bfloat16),
        ],
        compiler_params=pltpu.CompilerParams(vmem_limit_bytes=32 * 2**20),
        cost_estimate=pl.CostEstimate(
            flops=6 * work * height,
            bytes_accessed=4 * len(operands) * height * width,
            transcendentals=0,
        ),
        name="gram_chunk",
    )(*operands)


def final_chunk(index, z3, own, groups, previous, columns):
    rows = z3.shape[0]
    width = own.shape[1]
    pieces = z3.shape[1] // (3 * width)
    lists = [v for group in groups for v in group]
    first_row = index * lists[0].shape[0]
    steps = len(groups) * (lists[0].shape[0] // tile)
    anywhere = pl.BlockSpec(memory_space=pl.ANY)
    operands = [z3, own, *lists]
    specs = [pl.BlockSpec(z3.shape, lambda i: (0, 0), pipeline_mode=pl.Buffered(1))]
    specs += [anywhere] * (1 + len(lists))
    aliases = {}
    if previous is not None:
        aliases = {len(operands): 0}
        operands.append(previous)
        specs.append(anywhere)
    first_block = first_row // tile
    return pl.pallas_call(
        functools.partial(final_kernel, first_row, pieces, len(groups)),
        grid=(steps,),
        in_specs=specs,
        out_specs=pl.BlockSpec((rows, tile), lambda i: (0, first_block + i)),
        out_shape=jax.ShapeDtypeStruct((rows, columns), jnp.float32),
        scratch_shapes=[
            pltpu.VMEM((2, tile, pieces * width), jnp.float32),
            pltpu.VMEM((tile, 3 * pieces * width), jnp.bfloat16),
            pltpu.SemaphoreType.DMA((2, pieces)),
        ],
        input_output_aliases=aliases,
        compiler_params=pltpu.CompilerParams(vmem_limit_bytes=40 * 2**20),
        cost_estimate=pl.CostEstimate(
            flops=2 * rows * z3.shape[1] * steps * tile,
            bytes_accessed=4 * steps * tile * (rows + pieces * width),
            transcendentals=0,
        ),
        name="final_chunk",
    )(*operands)


MESH = pl.DeviceIdType.MESH


def send(source, target, send_sem, recv_sem, device):
    return pltpu.make_async_remote_copy(
        src_ref=source,
        dst_ref=target,
        send_sem=send_sem,
        recv_sem=recv_sem,
        device_id=device,
        device_id_type=MESH,
    )


def greet(device):
    pl.semaphore_signal(pltpu.get_barrier_semaphore(), inc=1, device_id=device, device_id_type=MESH)


def chain_kernel(
    chips, gram, table, eigen_j, eigen_i, ids_j, ids_i, slope_j, mine,
    met, total, came, w_tiles, w_high, w_low, zt, got, land,
    w_sems, met_send, met_recv, came_send, came_recv, z_send, z_recv,
):
    me = lax.axis_index("harm")
    layer = lax.axis_index("mode")
    core = lax.rem(me, 2)
    chip = lax.div(me, 2)
    partner = me + 1 - 2 * core
    middle = (layer == 1) | (layer == 2)
    span = met.shape[1]
    tiles, rows = w_tiles.shape[:2]
    peer = 3 - layer
    end = jnp.where(layer == 1, 0, 3)
    keep = jnp.where(layer == 1, 0, 2)
    slot = jnp.where(layer == 1, 0, 1)

    @pl.when(middle)
    def _():
        greet({"harm": partner})
        for d in range(1, chips):
            greet({"harm": lax.rem(chip + d, chips) * 2 + core})
        greet({"mode": layer - 1})
        greet({"mode": layer + 1})
        pl.semaphore_wait(pltpu.get_barrier_semaphore(), chips + 2)
        first = [
            send(
                gram.at[pl.ds((2 * q + 1 - core) * span, span), :],
                met.at[q],
                met_send.at[q],
                met_recv.at[q],
                {"harm": partner},
            )
            for q in range(chips)
        ]
        for copy in first:
            copy.start()
        loads = [
            pltpu.make_async_copy(table.at[pl.ds(t * rows, rows), :], w_tiles.at[t], w_sems.at[t])
            for t in range(tiles)
        ]
        for load in loads:
            load.start()
        for q in range(chips):
            first[q].wait()
            total[q] = gram[pl.ds((2 * q + core) * span, span), :] + met[q]
        second = []
        for d in range(1, chips):
            q = lax.rem(chip + d, chips)
            second.append(
                send(
                    total.at[q],
                    came.at[d - 1],
                    came_send.at[d - 1],
                    came_recv.at[d - 1],
                    {"harm": q * 2 + core},
                )
            )
            second[-1].start()
        for load in loads:
            load.wait()

        def cut(t, carry):
            high, low = split(w_tiles[t])
            w_high[t] = high
            w_low[t] = low
            return carry

        lax.fori_loop(0, tiles, cut, 0)
        for copy in second:
            copy.wait()
        value = total[chip]
        for d in range(1, chips):
            value = value + came[d - 1]
        differ = eigen_j[...] - eigen_i[...]
        value = value * (differ / (differ * differ + regular))
        value = value + jnp.where(ids_j[...] == ids_i[...], slope_j[...], 0.0)
        high, low = split(value)
        both = jnp.concatenate([high, low], axis=0)
        per = zt.shape[2] // rows
        nt = (((1,), (1,)), ((), ()))

        def mix(t, carry):
            part = lax.dot_general(both, w_high[t], nt, preferred_element_type=jnp.float32)
            rest = lax.dot_general(high, w_low[t], nt, preferred_element_type=jnp.float32)
            zt[t // per, :, pl.ds(pl.multiple_of(lax.rem(t, per) * rows, rows), rows)] = (
                part[:span] + part[span:] + rest
            )
            return carry

        lax.fori_loop(0, tiles, mix, 0)
        swap = send(zt.at[pl.ds(2 - keep, 2)], got, z_send.at[0], z_recv.at[0], {"mode": peer})
        swap.start()
        out = send(zt.at[end], land.at[slot], z_send.at[1], z_recv.at[1], {"mode": end})
        out.start()
        mine[slot] = zt[layer]
        swap.wait()
        pass_on = send(
            got.at[end - keep], land.at[1 - slot], z_send.at[2], z_recv.at[2], {"mode": end}
        )
        pass_on.start()
        mine[1 - slot] = got[layer - keep]
        out.wait_send()
        pass_on.wait_send()

    @pl.when(jnp.logical_not(middle))
    def _():
        inward = jnp.where(layer == 0, 1, 2)
        side = jnp.where(layer == 0, 0, 1)
        greet({"mode": inward})
        pl.semaphore_wait(pltpu.get_barrier_semaphore(), 1)
        send(zt.at[0], land.at[side], z_send.at[1], z_recv.at[1], {"mode": inward}).wait_recv()
        send(zt.at[0], land.at[1 - side], z_send.at[2], z_recv.at[2], {"mode": inward}).wait_recv()
        mine[...] = land[...]


def chain(gram, table, eigen_j, eigen_i, ids_j, ids_i, slope_j, harm_count, mode_count):
    chips = harm_count // 2
    span = gram.shape[0] // harm_count
    modes = gram.shape[1]
    rows = table.shape[0] // mode_count
    cut = 512
    tiles = table.shape[0] // cut
    vmem = pl.BlockSpec(memory_space=pltpu.VMEM)
    return pl.pallas_call(
        functools.partial(chain_kernel, chips),
        in_specs=[vmem, pl.BlockSpec(memory_space=pl.ANY)] + [vmem] * 5,
        out_specs=vmem,
        out_shape=jax.ShapeDtypeStruct((2, span, rows), jnp.float32),
        scratch_shapes=[
            pltpu.VMEM((chips, span, modes), jnp.float32),
            pltpu.VMEM((chips, span, modes), jnp.float32),
            pltpu.VMEM((chips - 1, span, modes), jnp.float32),
            pltpu.VMEM((tiles, cut, modes), jnp.float32),
            pltpu.VMEM((tiles, cut, modes), jnp.bfloat16),
            pltpu.VMEM((tiles, cut, modes), jnp.bfloat16),
            pltpu.VMEM((mode_count, span, rows), jnp.float32),
            pltpu.VMEM((2, span, rows), jnp.float32),
            pltpu.VMEM((2, span, rows), jnp.float32),
            pltpu.SemaphoreType.DMA((tiles,)),
            pltpu.SemaphoreType.DMA((chips,)),
            pltpu.SemaphoreType.DMA((chips,)),
            pltpu.SemaphoreType.DMA((chips - 1,)),
            pltpu.SemaphoreType.DMA((chips - 1,)),
            pltpu.SemaphoreType.DMA((3,)),
            pltpu.SemaphoreType.DMA((3,)),
        ],
        compiler_params=pltpu.CompilerParams(
            collective_id=1, has_side_effects=True, vmem_limit_bytes=52 * 2**20
        ),
        name="chain",
    )(gram, table, eigen_j, eigen_i, ids_j, ids_i, slope_j)


def spread_kernel(width, mine, z_ref, land, sends, recvs):
    me = lax.axis_index("harm")
    core = lax.rem(me, 2)
    chip = lax.div(me, 2)
    partner = me + 1 - 2 * core
    across = [chip + 1 - 2 * lax.rem(chip, 2), chip + 2 - 4 * lax.div(chip, 2)]
    opposite = 3 - chip
    greet({"harm": partner})
    for q in across:
        greet({"harm": q * 2 + core})
    pl.semaphore_wait(pltpu.get_barrier_semaphore(), 3)

    def push(source, origin, at, index, device):
        copy = send(source, land.at[origin, at], sends.at[index], recvs.at[index], {"harm": device})
        copy.start()
        return copy

    direct = [push(mine, chip, core, k, across[k] * 2 + core) for k in range(2)]
    pair = [push(mine, chip, core, 2, partner)]
    land[chip, core] = mine[...]
    relay = []
    for k in range(2):
        direct[k].wait()
        origin = across[k]
        relay.append(
            send(
                land.at[origin, core, k],
                land.at[origin, core, k],
                sends.at[3 + k],
                recvs.at[3 + k],
                {"harm": across[1 - k] * 2 + core},
            )
        )
        relay[k].start()
        pair.append(push(land.at[origin, core], origin, core, 5 + k, partner))
    for k in range(2):
        relay[k].wait()
    pair.append(push(land.at[opposite, core], opposite, core, 7, partner))
    for copy in pair:
        copy.wait()
    depth = z_ref.shape[1] // 3
    for q in range(4):
        for side in range(2):
            piece = 1 - q // 2 if side == 0 else 2 + q // 2
            block = jnp.concatenate([land[q, 0, side], land[q, 1, side]], axis=0).T
            high, low = split(block)
            size = block.shape[1]
            at = piece * width + (q % 2) * size
            z_ref[:, at : at + size] = high
            z_ref[:, depth + at : depth + at + size] = low
            z_ref[:, 2 * depth + at : 2 * depth + at + size] = high


def spread(mine, mode_count, width):
    vmem = pl.BlockSpec(memory_space=pltpu.VMEM)
    return pl.pallas_call(
        functools.partial(spread_kernel, width),
        in_specs=[vmem],
        out_specs=vmem,
        out_shape=jax.ShapeDtypeStruct((mine.shape[2], 3 * mode_count * width), jnp.bfloat16),
        scratch_shapes=[
            pltpu.VMEM((4, 2, *mine.shape), jnp.float32),
            pltpu.SemaphoreType.DMA((8,)),
            pltpu.SemaphoreType.DMA((8,)),
        ],
        compiler_params=pltpu.CompilerParams(
            collective_id=2, has_side_effects=True, vmem_limit_bytes=40 * 2**20
        ),
        name="spread",
    )(mine)


def slab_order(slab_rows, row_count, harm_count, harm_index):
    total = slab_rows.shape[0]
    share = total // harm_count
    owner = slab_rows // row_count
    ids = lax.broadcasted_iota(jnp.int32, (harm_count, total), 0)
    hit = (owner[None, :] == ids).astype(jnp.int32)
    running = jnp.cumsum(hit, axis=1)
    rank = jnp.sum(hit * running, axis=0) - 1
    position = owner * share + rank
    slots = lax.broadcasted_iota(jnp.int32, (share, total), 0)
    mine = (position - harm_index * share)[None, :] == slots
    offsets = jnp.sum(jnp.where(mine, (slab_rows - harm_index * row_count)[None, :], 0), axis=1)
    return position, offsets


def line_body(mode_vectors, weights, cotangent, eigenvalues, eigen_cotangent, slab_rows, harm_count, mode_count):
    harm = lax.axis_index("harm")
    layer = lax.axis_index("mode")
    height, width = mode_vectors.shape
    lower = layer <= 1
    part = height // chunks
    own = [mode_vectors[:part]]
    rest, first = lax.optimization_barrier((mode_vectors, own[0]))
    own = [first] + [rest[c * part : (c + 1) * part] for c in range(1, chunks)]
    slope = jnp.split(cotangent, chunks, 0)

    def hop(values, pairs):
        results = []
        for value in values:
            results.append(shift(value, pairs))
        return results

    b1 = hop(own, [(0, 1), (1, 2), (2, 3)])
    a1 = hop(own, [(1, 0), (2, 1), (3, 2)])

    position, offsets = slab_order(slab_rows, height, harm_count, harm)
    picked = jnp.take(weights, offsets, axis=0, mode="clip")
    w_b1 = shift(picked, [(0, 1), (1, 2)])
    w_a1 = shift(picked, [(3, 2), (2, 1)])
    w_third = shift(w_b1, [(1, 2)]) + shift(w_a1, [(2, 1)])
    w_all = jnp.concatenate([picked, w_b1, w_a1, w_third], axis=1)
    w_every = lax.all_gather(w_all, "harm", axis=0, tiled=True)
    w_slab = jnp.take(w_every, position, axis=0, mode="clip")

    b2 = hop(b1, [(1, 2), (2, 3)])
    a2 = hop(a1, [(2, 1), (1, 0)])
    edge = hop(slope, [(0, 1), (3, 2)])
    b3 = hop(b2, [(2, 3)])
    a3 = hop(a2, [(1, 0)])

    near = None
    for c in range(chunks):
        near = gram_chunk(
            c, part, [cotangent], [mode_vectors, b1[c], a1[c]], (1, 1, 1),
            ((0, 0),), ((width, 3 * width),), near,
        )
    far_parts = None
    for c in range(chunks):
        side = edge[c]
        if c == 2:
            side, w_slab = lax.optimization_barrier((side, w_slab))
        far_parts = gram_chunk(
            c, part, [cotangent, side], [mode_vectors, b1[c], a1[c], b2[c], a2[c]], (1, 1, 1, 1, 0),
            ((0, 3 * width), (width, 0)), ((width, width), (width, 4 * width)), far_parts,
        )
    top = jnp.concatenate([near[0], far_parts[0]], axis=1)
    gram = jnp.concatenate([top, far_parts[1]], axis=0)

    span = 2 * width // harm_count
    half = harm_count // 2
    last = mode_count - 1
    end = jnp.where(lower, 0, last)
    far = jnp.where(lower, last, 0)
    first_col = jnp.where(harm < half, layer * width + harm * span, end * width + (harm - half) * span)
    blocks = [layer, jnp.maximum(layer - 1, 0), jnp.minimum(layer + 1, last), far]
    row_ids = jnp.concatenate([b * width + jnp.arange(width, dtype=jnp.int32) for b in blocks])
    eigen_i = jnp.concatenate([lax.dynamic_slice_in_dim(eigenvalues, b * width, width) for b in blocks])
    eigen_j = lax.dynamic_slice_in_dim(eigenvalues, first_col, span)
    slope_j = lax.dynamic_slice_in_dim(eigen_cotangent, first_col, span)
    col_ids = first_col + jnp.arange(span, dtype=jnp.int32)
    mine = chain(
        gram, w_slab, eigen_j[:, None], eigen_i[None, :], col_ids[:, None], row_ids[None, :],
        slope_j[:, None], harm_count, mode_count,
    )
    z3 = spread(mine, mode_count, width)

    out = None
    lists = list(zip(b1, b2, b3, a1, a2, a3))
    for first, count in ((0, 2), (2, 1), (3, 1)):
        out = final_chunk(first, z3, mode_vectors, lists[first : first + count], out, height)
    return out


def line(*operands):
    return line_body(*operands)


def solution(mesh):
    harm_count = mesh.shape["harm"]
    mode_count = mesh.shape["mode"]
    placed = (P("harm", "mode"), P("harm", "mode"), P("harm", "mode"), P(), P(), P())
    lined = mode_count == 4 and harm_count == 8
    form = line if lined else plain

    def local(*operands):
        return form(*operands, harm_count, mode_count)

    return jax.shard_map(
        local, mesh=mesh, in_specs=placed, out_specs=P("mode", "harm"), check_vma=False
    )
```

```python
import functools

import jax
import jax.numpy as jnp
from jax import lax
from jax.experimental import pallas as pl
from jax.experimental.pallas import tpu as pltpu
from jax.sharding import PartitionSpec as P


regular = 0.01
chunks = 4
tile = 512


def product(left, right, left_dim, right_dim):
    return lax.dot_general(
        left,
        right,
        (((left_dim,), (right_dim,)), ((), ())),
        precision=lax.Precision.HIGH,
        preferred_element_type=jnp.float32,
    )


def weigh_gap(block, row_ids, col_ids, eigenvalues, eigen_cotangent):
    eigen_rows = lax.dynamic_slice_in_dim(eigenvalues, row_ids, block.shape[0])
    eigen_cols = lax.dynamic_slice_in_dim(eigenvalues, col_ids, block.shape[1])
    slope_cols = lax.dynamic_slice_in_dim(eigen_cotangent, col_ids, block.shape[1])
    differ = eigen_cols[None, :] - eigen_rows[:, None]
    factor = differ / (differ * differ + regular)
    rows = row_ids + lax.broadcasted_iota(jnp.int32, block.shape, 0)
    cols = col_ids + lax.broadcasted_iota(jnp.int32, block.shape, 1)
    return factor * block + jnp.where(rows == cols, slope_cols[None, :], 0.0)


def pick_rows(table, slab_rows, harm_index):
    row_count = table.shape[0]
    offset = slab_rows - harm_index * row_count
    inside = (offset >= 0) & (offset < row_count)
    picked = jnp.take(table, jnp.clip(offset, 0, row_count - 1), axis=0)
    return jnp.where(inside[:, None], picked, 0.0)


def gather_weights(weights, slab_rows, harm_index, harm_count, mode_count):
    width = weights.shape[1]
    picked = pick_rows(weights, slab_rows, harm_index)
    piece = slab_rows.shape[0] // (harm_count * mode_count)
    picked = picked.reshape(mode_count, harm_count, piece, width)
    picked = lax.psum_scatter(picked, "harm", scatter_dimension=1, tiled=True)
    picked = picked.reshape(mode_count, piece, width)
    swapped = lax.all_to_all(picked, "mode", split_axis=0, concat_axis=2, tiled=True)
    return lax.all_gather(swapped.reshape(piece, mode_count * width), "harm", axis=0, tiled=True)


def plain(mode_vectors, weights, cotangent, eigenvalues, eigen_cotangent, slab_rows, harm_count, mode_count):
    harm_index = lax.axis_index("harm")
    width = mode_vectors.shape[1]
    modes = width * mode_count
    full = lax.all_gather(mode_vectors, "mode", axis=1, tiled=True)
    owned_weights = gather_weights(weights, slab_rows, harm_index, harm_count, mode_count)
    gram = product(full, cotangent, 0, 0)
    gram = lax.psum_scatter(gram, "harm", scatter_dimension=0, tiled=True)
    weighted = weigh_gap(
        gram,
        harm_index * (modes // harm_count),
        lax.axis_index("mode") * width,
        eigenvalues,
        eigen_cotangent,
    )
    weighted = lax.all_gather(weighted, "mode", axis=1, tiled=True)
    weighted = lax.all_gather(weighted, "harm", axis=0, tiled=True)
    return product(product(owned_weights, weighted, 1, 0), full, 1, 1)


def shift(value, pairs):
    return lax.ppermute(value, "mode", pairs)


def split(value):
    high = value.astype(jnp.bfloat16)
    low = (value - high.astype(jnp.float32)).astype(jnp.bfloat16)
    return high, low


def final_kernel(first_row, pieces, parts, z_ref, own, *rest):
    lists = [rest[6 * c : 6 * c + 6] for c in range(parts)]
    out_ref, x_buf, x3, sems = rest[-4:]
    step = pl.program_id(0)
    steps = pl.num_programs(0)
    each = steps // parts
    layer = lax.axis_index("mode")
    width = own.shape[1]
    rows = x_buf.shape[1]

    def fetch(at, slot, chosen):
        for c in chosen:
            for piece in range(pieces):
                for here in range(pieces):
                    delta = piece - here

                    @pl.when((layer == here) & (at >= c * each) & (at < (c + 1) * each))
                    def _():
                        if delta == 0:
                            source, begin = own, first_row + at * rows
                        else:
                            source = lists[c][2 + delta if delta > 0 else -delta - 1]
                            begin = (at - c * each) * rows
                        pltpu.make_async_copy(
                            source.at[pl.ds(begin, rows), :],
                            x_buf.at[slot, :, pl.ds(piece * width, width)],
                            sems.at[slot, piece],
                        ).start()

    slot = lax.rem(step, 2)

    @pl.when(step == 0)
    def _():
        fetch(step, 0, (0,))

    @pl.when(step + 1 < steps)
    def _():
        fetch(step + 1, 1 - slot, range(parts))

    for piece in range(pieces):
        pltpu.make_async_copy(
            own.at[pl.ds(0, rows), :],
            x_buf.at[slot, :, pl.ds(piece * width, width)],
            sems.at[slot, piece],
        ).wait()
    depth = x_buf.shape[2]
    high, low = split(x_buf[slot])
    x3[:, :depth] = high
    x3[:, depth : 2 * depth] = high
    x3[:, 2 * depth :] = low
    out_ref[...] = lax.dot_general(
        z_ref[...], x3[...], (((1,), (1,)), ((), ())), preferred_element_type=jnp.float32
    )


def gram_kernel(lefts, rights, plan, *refs):
    sides = refs[: lefts + len(rights)]
    count = len(plan)
    outs = refs[-2 - count : -2]
    seeds = refs[lefts + len(rights) : -2 - count]
    left3, right3 = refs[-2:]
    rows = sides[0].shape[0]
    slots = [sum(rights[:i]) for i in range(len(rights))]

    @pl.when(pl.program_id(0) == 0)
    def _():
        for index, out in enumerate(outs):
            out[...] = seeds[index][...] if seeds else jnp.zeros_like(out)

    for index in range(lefts):
        width = sides[index].shape[1]
        high, low = split(sides[index][...])
        at = pl.ds(index * width, width)
        left3[:rows, at] = high
        left3[rows : 2 * rows, at] = low
        left3[2 * rows :, at] = high
    for index, fresh in enumerate(rights):
        if not fresh:
            continue
        value = sides[lefts + index][...]
        if index + 1 < len(rights) and not rights[index + 1]:
            value = value + sides[lefts + index + 1][...]
        width = value.shape[1]
        high, low = split(value)
        at = pl.ds(slots[index] * width, width)
        right3[:rows, at] = high
        right3[rows : 2 * rows, at] = high
        right3[2 * rows :, at] = low
    for out, (row, col) in zip(outs, plan):
        high, wide = out.shape
        out[...] += lax.dot_general(
            left3[:, row : row + high],
            right3[:, col : col + wide],
            (((0,), (0,)), ((), ())),
            preferred_element_type=jnp.float32,
        )


def gram_chunk(index, height, lefts, rights, fresh, plan, shapes, seeds):
    width = lefts[0].shape[1]
    steps = height // tile
    first = index * steps
    whole = pl.BlockSpec((tile, width), lambda i: (first + i, 0))
    part = pl.BlockSpec((tile, width), lambda i: (i, 0))
    specs = [part if v.shape[0] == height else whole for v in (*lefts, *rights)]
    fixed = [pl.BlockSpec(s, lambda i: (0, 0)) for s in shapes]
    work = sum(s[0] * s[1] for s in shapes)
    operands = [*lefts, *rights]
    if seeds is not None:
        operands += seeds
        specs += fixed
    return pl.pallas_call(
        functools.partial(gram_kernel, len(lefts), fresh, plan),
        grid=(steps,),
        in_specs=specs,
        out_specs=fixed,
        out_shape=[jax.ShapeDtypeStruct(s, jnp.float32) for s in shapes],
        scratch_shapes=[
            pltpu.VMEM((3 * tile, len(lefts) * width), jnp.bfloat16),
            pltpu.VMEM((3 * tile, sum(fresh) * width), jnp.bfloat16),
        ],
        compiler_params=pltpu.CompilerParams(vmem_limit_bytes=32 * 2**20),
        cost_estimate=pl.CostEstimate(
            flops=6 * work * height,
            bytes_accessed=4 * len(operands) * height * width,
            transcendentals=0,
        ),
        name="gram_chunk",
    )(*operands)


def final_chunk(index, z3, own, groups, previous, columns):
    rows = z3.shape[0]
    width = own.shape[1]
    pieces = z3.shape[1] // (3 * width)
    lists = [v for group in groups for v in group]
    first_row = index * lists[0].shape[0]
    steps = len(groups) * (lists[0].shape[0] // tile)
    anywhere = pl.BlockSpec(memory_space=pl.ANY)
    operands = [z3, own, *lists]
    specs = [pl.BlockSpec(z3.shape, lambda i: (0, 0), pipeline_mode=pl.Buffered(1))]
    specs += [anywhere] * (1 + len(lists))
    aliases = {}
    if previous is not None:
        aliases = {len(operands): 0}
        operands.append(previous)
        specs.append(anywhere)
    first_block = first_row // tile
    return pl.pallas_call(
        functools.partial(final_kernel, first_row, pieces, len(groups)),
        grid=(steps,),
        in_specs=specs,
        out_specs=pl.BlockSpec((rows, tile), lambda i: (0, first_block + i)),
        out_shape=jax.ShapeDtypeStruct((rows, columns), jnp.float32),
        scratch_shapes=[
            pltpu.VMEM((2, tile, pieces * width), jnp.float32),
            pltpu.VMEM((tile, 3 * pieces * width), jnp.bfloat16),
            pltpu.SemaphoreType.DMA((2, pieces)),
        ],
        input_output_aliases=aliases,
        compiler_params=pltpu.CompilerParams(vmem_limit_bytes=40 * 2**20),
        cost_estimate=pl.CostEstimate(
            flops=2 * rows * z3.shape[1] * steps * tile,
            bytes_accessed=4 * steps * tile * (rows + pieces * width),
            transcendentals=0,
        ),
        name="final_chunk",
    )(*operands)


MESH = pl.DeviceIdType.MESH


def send(source, target, send_sem, recv_sem, device):
    return pltpu.make_async_remote_copy(
        src_ref=source,
        dst_ref=target,
        send_sem=send_sem,
        recv_sem=recv_sem,
        device_id=device,
        device_id_type=MESH,
    )


def greet(device):
    pl.semaphore_signal(pltpu.get_barrier_semaphore(), inc=1, device_id=device, device_id_type=MESH)


def order_kernel(count, position, *refs):
    blocks = refs[:count]
    high_ref, low_ref, buf, stage, sems = refs[count:]
    step = pl.program_id(0)
    share = blocks[0].shape[0]
    rows = stage.shape[0]

    @pl.when(step == 0)
    def _():
        copies = [
            pltpu.make_async_copy(blocks[k], buf.at[pl.ds(k * share, share), :], sems.at[k])
            for k in range(count)
        ]
        for copy in copies:
            copy.start()
        for copy in copies:
            copy.wait()

    def body(index, carry):
        base = index * 8
        for k in range(8):
            stage[pl.ds(base + k, 1), :] = buf[pl.ds(position[step * rows + base + k], 1), :]
        return carry

    lax.fori_loop(0, rows // 8, body, 0)
    high, low = split(stage[...])
    high_ref[0] = high
    low_ref[0] = low


def order(position, blocks):
    share, modes = blocks[0].shape
    count = len(blocks)
    rows = 512
    steps = count * share // rows
    shape = jax.ShapeDtypeStruct((steps, rows, modes), jnp.bfloat16)
    spec = pl.BlockSpec((1, rows, modes), lambda i, p: (i, 0, 0))
    return pl.pallas_call(
        functools.partial(order_kernel, count),
        grid_spec=pltpu.PrefetchScalarGridSpec(
            num_scalar_prefetch=1,
            grid=(steps,),
            in_specs=[pl.BlockSpec(memory_space=pl.ANY)] * count,
            out_specs=[spec, spec],
            scratch_shapes=[
                pltpu.VMEM((count * share, modes), jnp.float32),
                pltpu.VMEM((rows, modes), jnp.float32),
                pltpu.SemaphoreType.DMA((count,)),
            ],
        ),
        out_shape=[shape, shape],
        compiler_params=pltpu.CompilerParams(vmem_limit_bytes=32 * 2**20),
        cost_estimate=pl.CostEstimate(
            flops=0, bytes_accessed=8 * count * share * modes, transcendentals=0
        ),
        name="order",
    )(position, *blocks)


def chain_kernel(
    chips, gram, high_table, low_table, eigen_j, eigen_i, ids_j, ids_i, slope_j, mine,
    met, total, came, w_high, w_low, zt, got, land,
    w_sems, met_send, met_recv, came_send, came_recv, z_send, z_recv,
):
    me = lax.axis_index("harm")
    layer = lax.axis_index("mode")
    core = lax.rem(me, 2)
    chip = lax.div(me, 2)
    partner = me + 1 - 2 * core
    middle = (layer == 1) | (layer == 2)
    span = met.shape[1]
    tiles, rows = w_high.shape[:2]
    peer = 3 - layer
    end = jnp.where(layer == 1, 0, 3)
    keep = jnp.where(layer == 1, 0, 2)
    slot = jnp.where(layer == 1, 0, 1)

    @pl.when(middle)
    def _():
        greet({"harm": partner})
        for d in range(1, chips):
            greet({"harm": lax.rem(chip + d, chips) * 2 + core})
        greet({"mode": layer - 1})
        greet({"mode": layer + 1})
        pl.semaphore_wait(pltpu.get_barrier_semaphore(), chips + 2)
        first = [
            send(
                gram.at[pl.ds((2 * q + 1 - core) * span, span), :],
                met.at[q],
                met_send.at[q],
                met_recv.at[q],
                {"harm": partner},
            )
            for q in range(chips)
        ]
        for copy in first:
            copy.start()
        loads = [
            pltpu.make_async_copy(high_table, w_high, w_sems.at[0]),
            pltpu.make_async_copy(low_table, w_low, w_sems.at[1]),
        ]
        for load in loads:
            load.start()
        for q in range(chips):
            first[q].wait()
            total[q] = gram[pl.ds((2 * q + core) * span, span), :] + met[q]
        second = []
        for d in range(1, chips):
            q = lax.rem(chip + d, chips)
            second.append(
                send(
                    total.at[q],
                    came.at[d - 1],
                    came_send.at[d - 1],
                    came_recv.at[d - 1],
                    {"harm": q * 2 + core},
                )
            )
            second[-1].start()
        for load in loads:
            load.wait()
        for copy in second:
            copy.wait()
        value = total[chip]
        for d in range(1, chips):
            value = value + came[d - 1]
        differ = eigen_j[...] - eigen_i[...]
        value = value * (differ / (differ * differ + regular))
        value = value + jnp.where(ids_j[...] == ids_i[...], slope_j[...], 0.0)
        high, low = split(value)
        both = jnp.concatenate([high, low], axis=0)
        per = zt.shape[2] // rows
        nt = (((1,), (1,)), ((), ()))

        def mix(t, carry):
            part = lax.dot_general(both, w_high[t], nt, preferred_element_type=jnp.float32)
            rest = lax.dot_general(high, w_low[t], nt, preferred_element_type=jnp.float32)
            zt[t // per, :, pl.ds(pl.multiple_of(lax.rem(t, per) * rows, rows), rows)] = (
                part[:span] + part[span:] + rest
            )
            return carry

        lax.fori_loop(0, tiles, mix, 0)
        swap = send(zt.at[pl.ds(2 - keep, 2)], got, z_send.at[0], z_recv.at[0], {"mode": peer})
        swap.start()
        out = send(zt.at[end], land.at[slot], z_send.at[1], z_recv.at[1], {"mode": end})
        out.start()
        mine[slot] = zt[layer]
        swap.wait()
        pass_on = send(
            got.at[end - keep], land.at[1 - slot], z_send.at[2], z_recv.at[2], {"mode": end}
        )
        pass_on.start()
        mine[1 - slot] = got[layer - keep]
        out.wait_send()
        pass_on.wait_send()

    @pl.when(jnp.logical_not(middle))
    def _():
        inward = jnp.where(layer == 0, 1, 2)
        side = jnp.where(layer == 0, 0, 1)
        greet({"mode": inward})
        pl.semaphore_wait(pltpu.get_barrier_semaphore(), 1)
        send(zt.at[0], land.at[side], z_send.at[1], z_recv.at[1], {"mode": inward}).wait_recv()
        send(zt.at[0], land.at[1 - side], z_send.at[2], z_recv.at[2], {"mode": inward}).wait_recv()
        mine[...] = land[...]


def chain(gram, high_table, low_table, eigen_j, eigen_i, ids_j, ids_i, slope_j, harm_count, mode_count):
    chips = harm_count // 2
    span = gram.shape[0] // harm_count
    modes = gram.shape[1]
    rows = high_table.shape[0] * high_table.shape[1] // mode_count
    vmem = pl.BlockSpec(memory_space=pltpu.VMEM)
    return pl.pallas_call(
        functools.partial(chain_kernel, chips),
        in_specs=[vmem] + [pl.BlockSpec(memory_space=pl.ANY)] * 2 + [vmem] * 5,
        out_specs=vmem,
        out_shape=jax.ShapeDtypeStruct((2, span, rows), jnp.float32),
        scratch_shapes=[
            pltpu.VMEM((chips, span, modes), jnp.float32),
            pltpu.VMEM((chips, span, modes), jnp.float32),
            pltpu.VMEM((chips - 1, span, modes), jnp.float32),
            pltpu.VMEM(high_table.shape, jnp.bfloat16),
            pltpu.VMEM(low_table.shape, jnp.bfloat16),
            pltpu.VMEM((mode_count, span, rows), jnp.float32),
            pltpu.VMEM((2, span, rows), jnp.float32),
            pltpu.VMEM((2, span, rows), jnp.float32),
            pltpu.SemaphoreType.DMA((2,)),
            pltpu.SemaphoreType.DMA((chips,)),
            pltpu.SemaphoreType.DMA((chips,)),
            pltpu.SemaphoreType.DMA((chips - 1,)),
            pltpu.SemaphoreType.DMA((chips - 1,)),
            pltpu.SemaphoreType.DMA((3,)),
            pltpu.SemaphoreType.DMA((3,)),
        ],
        compiler_params=pltpu.CompilerParams(
            collective_id=1, has_side_effects=True, vmem_limit_bytes=52 * 2**20
        ),
        name="chain",
    )(gram, high_table, low_table, eigen_j, eigen_i, ids_j, ids_i, slope_j)


def spread_kernel(width, mine, z_ref, land, sends, recvs):
    me = lax.axis_index("harm")
    core = lax.rem(me, 2)
    chip = lax.div(me, 2)
    partner = me + 1 - 2 * core
    across = [chip + 1 - 2 * lax.rem(chip, 2), chip + 2 - 4 * lax.div(chip, 2)]
    opposite = 3 - chip
    greet({"harm": partner})
    for q in across:
        greet({"harm": q * 2 + core})
    pl.semaphore_wait(pltpu.get_barrier_semaphore(), 3)

    def push(source, origin, at, index, device):
        copy = send(source, land.at[origin, at], sends.at[index], recvs.at[index], {"harm": device})
        copy.start()
        return copy

    direct = [push(mine, chip, core, k, across[k] * 2 + core) for k in range(2)]
    pair = [push(mine, chip, core, 2, partner)]
    land[chip, core] = mine[...]
    relay = []
    for k in range(2):
        direct[k].wait()
        origin = across[k]
        relay.append(
            send(
                land.at[origin, core, k],
                land.at[origin, core, k],
                sends.at[3 + k],
                recvs.at[3 + k],
                {"harm": across[1 - k] * 2 + core},
            )
        )
        relay[k].start()
        pair.append(push(land.at[origin, core], origin, core, 5 + k, partner))
    for k in range(2):
        relay[k].wait()
    pair.append(push(land.at[opposite, core], opposite, core, 7, partner))
    for copy in pair:
        copy.wait()
    depth = z_ref.shape[1] // 3
    for q in range(4):
        for side in range(2):
            piece = 1 - q // 2 if side == 0 else 2 + q // 2
            block = jnp.concatenate([land[q, 0, side], land[q, 1, side]], axis=0).T
            high, low = split(block)
            size = block.shape[1]
            at = piece * width + (q % 2) * size
            z_ref[:, at : at + size] = high
            z_ref[:, depth + at : depth + at + size] = low
            z_ref[:, 2 * depth + at : 2 * depth + at + size] = high


def spread(mine, mode_count, width):
    vmem = pl.BlockSpec(memory_space=pltpu.VMEM)
    return pl.pallas_call(
        functools.partial(spread_kernel, width),
        in_specs=[vmem],
        out_specs=vmem,
        out_shape=jax.ShapeDtypeStruct((mine.shape[2], 3 * mode_count * width), jnp.bfloat16),
        scratch_shapes=[
            pltpu.VMEM((4, 2, *mine.shape), jnp.float32),
            pltpu.SemaphoreType.DMA((8,)),
            pltpu.SemaphoreType.DMA((8,)),
        ],
        compiler_params=pltpu.CompilerParams(
            collective_id=2, has_side_effects=True, vmem_limit_bytes=40 * 2**20
        ),
        name="spread",
    )(mine)


def slab_order(slab_rows, row_count, harm_count, harm_index):
    total = slab_rows.shape[0]
    share = total // harm_count
    owner = slab_rows // row_count
    ids = lax.broadcasted_iota(jnp.int32, (harm_count, total), 0)
    hit = (owner[None, :] == ids).astype(jnp.int32)
    running = jnp.cumsum(hit, axis=1)
    rank = jnp.sum(hit * running, axis=0) - 1
    position = (owner ^ harm_index) * share + rank
    slots = lax.broadcasted_iota(jnp.int32, (share, total), 0)
    mine = position[None, :] == slots
    offsets = jnp.sum(jnp.where(mine, (slab_rows - harm_index * row_count)[None, :], 0), axis=1)
    return position, offsets


def line_body(mode_vectors, weights, cotangent, eigenvalues, eigen_cotangent, slab_rows, harm_count, mode_count):
    harm = lax.axis_index("harm")
    layer = lax.axis_index("mode")
    height, width = mode_vectors.shape
    lower = layer <= 1
    part = height // chunks
    own = [mode_vectors[:part]]
    rest, first = lax.optimization_barrier((mode_vectors, own[0]))
    own = [first] + [rest[c * part : (c + 1) * part] for c in range(1, chunks)]
    slope = jnp.split(cotangent, chunks, 0)

    def hop(values, pairs):
        results = []
        for value in values:
            results.append(shift(value, pairs))
        return results

    b1 = hop(own, [(0, 1), (1, 2), (2, 3)])
    a1 = hop(own, [(1, 0), (2, 1), (3, 2)])

    position, offsets = slab_order(slab_rows, height, harm_count, harm)
    picked = jnp.take(weights, offsets, axis=0, mode="clip")
    w_b1 = shift(picked, [(0, 1), (1, 2)])
    w_a1 = shift(picked, [(3, 2), (2, 1)])
    w_third = shift(w_b1, [(1, 2)]) + shift(w_a1, [(2, 1)])
    w_all = jnp.concatenate([picked, w_b1, w_a1, w_third], axis=1)
    pairs = lambda flip: [(n, n ^ flip) for n in range(harm_count)]
    blocks = [w_all] + [lax.ppermute(w_all, "harm", pairs(2 * d)) for d in (1, 2, 3)]
    blocks = [v for block in blocks for v in (block, lax.ppermute(block, "harm", pairs(1)))]
    w_high, w_low = order(position, blocks)

    b2 = hop(b1, [(1, 2), (2, 3)])
    a2 = hop(a1, [(2, 1), (1, 0)])
    edge = hop(slope, [(0, 1), (3, 2)])
    b3 = hop(b2, [(2, 3)])
    a3 = hop(a2, [(1, 0)])

    near = None
    for c in range(chunks):
        near = gram_chunk(
            c, part, [cotangent], [mode_vectors, b1[c], a1[c]], (1, 1, 1),
            ((0, 0),), ((width, 3 * width),), near,
        )
    far_parts = None
    for c in range(chunks):
        side = edge[c]
        if c == 1:
            side, w_high, w_low = lax.optimization_barrier((side, w_high, w_low))
        far_parts = gram_chunk(
            c, part, [cotangent, side], [mode_vectors, b1[c], a1[c], b2[c], a2[c]], (1, 1, 1, 1, 0),
            ((0, 3 * width), (width, 0)), ((width, width), (width, 4 * width)), far_parts,
        )
    top = jnp.concatenate([near[0], far_parts[0]], axis=1)
    gram = jnp.concatenate([top, far_parts[1]], axis=0)

    span = 2 * width // harm_count
    half = harm_count // 2
    last = mode_count - 1
    end = jnp.where(lower, 0, last)
    far = jnp.where(lower, last, 0)
    first_col = jnp.where(harm < half, layer * width + harm * span, end * width + (harm - half) * span)
    blocks = [layer, jnp.maximum(layer - 1, 0), jnp.minimum(layer + 1, last), far]
    row_ids = jnp.concatenate([b * width + jnp.arange(width, dtype=jnp.int32) for b in blocks])
    eigen_i = jnp.concatenate([lax.dynamic_slice_in_dim(eigenvalues, b * width, width) for b in blocks])
    eigen_j = lax.dynamic_slice_in_dim(eigenvalues, first_col, span)
    slope_j = lax.dynamic_slice_in_dim(eigen_cotangent, first_col, span)
    col_ids = first_col + jnp.arange(span, dtype=jnp.int32)
    mine = chain(
        gram, w_high, w_low, eigen_j[:, None], eigen_i[None, :], col_ids[:, None], row_ids[None, :],
        slope_j[:, None], harm_count, mode_count,
    )
    z3 = spread(mine, mode_count, width)

    out = None
    lists = list(zip(b1, b2, b3, a1, a2, a3))
    for first, count in ((0, chunks - 1), (chunks - 1, 1)):
        out = final_chunk(first, z3, mode_vectors, lists[first : first + count], out, height)
    return out


def line(*operands):
    return line_body(*operands)


def solution(mesh):
    harm_count = mesh.shape["harm"]
    mode_count = mesh.shape["mode"]
    placed = (P("harm", "mode"), P("harm", "mode"), P("harm", "mode"), P(), P(), P())
    lined = mode_count == 4 and harm_count == 8
    form = line if lined else plain

    def local(*operands):
        return form(*operands, harm_count, mode_count)

    return jax.shard_map(
        local, mesh=mesh, in_specs=placed, out_specs=P("mode", "harm"), check_vma=False
    )
```

```python
import functools

import jax
import jax.numpy as jnp
from jax import lax
from jax.experimental import pallas as pl
from jax.experimental.pallas import tpu as pltpu
from jax.sharding import PartitionSpec as P


regular = 0.01
chunks = 4
tile = 512
final_tile = 768


def product(left, right, left_dim, right_dim):
    return lax.dot_general(
        left,
        right,
        (((left_dim,), (right_dim,)), ((), ())),
        precision=lax.Precision.HIGH,
        preferred_element_type=jnp.float32,
    )


def weigh_gap(block, row_ids, col_ids, eigenvalues, eigen_cotangent):
    eigen_rows = lax.dynamic_slice_in_dim(eigenvalues, row_ids, block.shape[0])
    eigen_cols = lax.dynamic_slice_in_dim(eigenvalues, col_ids, block.shape[1])
    slope_cols = lax.dynamic_slice_in_dim(eigen_cotangent, col_ids, block.shape[1])
    differ = eigen_cols[None, :] - eigen_rows[:, None]
    factor = differ / (differ * differ + regular)
    rows = row_ids + lax.broadcasted_iota(jnp.int32, block.shape, 0)
    cols = col_ids + lax.broadcasted_iota(jnp.int32, block.shape, 1)
    return factor * block + jnp.where(rows == cols, slope_cols[None, :], 0.0)


def pick_rows(table, slab_rows, harm_index):
    row_count = table.shape[0]
    offset = slab_rows - harm_index * row_count
    inside = (offset >= 0) & (offset < row_count)
    picked = jnp.take(table, jnp.clip(offset, 0, row_count - 1), axis=0)
    return jnp.where(inside[:, None], picked, 0.0)


def gather_weights(weights, slab_rows, harm_index, harm_count, mode_count):
    width = weights.shape[1]
    picked = pick_rows(weights, slab_rows, harm_index)
    piece = slab_rows.shape[0] // (harm_count * mode_count)
    picked = picked.reshape(mode_count, harm_count, piece, width)
    picked = lax.psum_scatter(picked, "harm", scatter_dimension=1, tiled=True)
    picked = picked.reshape(mode_count, piece, width)
    swapped = lax.all_to_all(picked, "mode", split_axis=0, concat_axis=2, tiled=True)
    return lax.all_gather(swapped.reshape(piece, mode_count * width), "harm", axis=0, tiled=True)


def plain(mode_vectors, weights, cotangent, eigenvalues, eigen_cotangent, slab_rows, harm_count, mode_count):
    harm_index = lax.axis_index("harm")
    width = mode_vectors.shape[1]
    modes = width * mode_count
    full = lax.all_gather(mode_vectors, "mode", axis=1, tiled=True)
    owned_weights = gather_weights(weights, slab_rows, harm_index, harm_count, mode_count)
    gram = product(full, cotangent, 0, 0)
    gram = lax.psum_scatter(gram, "harm", scatter_dimension=0, tiled=True)
    weighted = weigh_gap(
        gram,
        harm_index * (modes // harm_count),
        lax.axis_index("mode") * width,
        eigenvalues,
        eigen_cotangent,
    )
    weighted = lax.all_gather(weighted, "mode", axis=1, tiled=True)
    weighted = lax.all_gather(weighted, "harm", axis=0, tiled=True)
    return product(product(owned_weights, weighted, 1, 0), full, 1, 1)


def shift(value, pairs):
    return lax.ppermute(value, "mode", pairs)


def split(value):
    high = value.astype(jnp.bfloat16)
    low = (value - high.astype(jnp.float32)).astype(jnp.bfloat16)
    return high, low


def final_kernel(first_row, pieces, parts, z_hbm, own, *rest):
    lists = [rest[6 * c : 6 * c + 6] for c in range(parts)]
    out_ref, x_buf, x3, z_ref, z_sem, sems = rest[-6:]
    step = pl.program_id(0)
    steps = pl.num_programs(0)
    each = steps // parts
    layer = lax.axis_index("mode")
    width = own.shape[1]
    rows = x_buf.shape[1]

    def fetch(at, slot, chosen):
        for c in chosen:
            for piece in range(pieces):
                for here in range(pieces):
                    delta = piece - here

                    @pl.when((layer == here) & (at >= c * each) & (at < (c + 1) * each))
                    def _():
                        if delta == 0:
                            source, begin = own, first_row + at * rows
                        else:
                            source = lists[c][2 + delta if delta > 0 else -delta - 1]
                            begin = (at - c * each) * rows
                        pltpu.make_async_copy(
                            source.at[pl.ds(begin, rows), :],
                            x_buf.at[slot, :, pl.ds(piece * width, width)],
                            sems.at[slot, piece],
                        ).start()

    slot = lax.rem(step, 2)

    @pl.when(step == 0)
    def _():
        fetch(step, 0, (0,))
        pltpu.make_async_copy(z_hbm, z_ref, z_sem).start()

    @pl.when(step + 1 < steps)
    def _():
        fetch(step + 1, 1 - slot, range(parts))

    for piece in range(pieces):
        pltpu.make_async_copy(
            own.at[pl.ds(0, rows), :],
            x_buf.at[slot, :, pl.ds(piece * width, width)],
            sems.at[slot, piece],
        ).wait()
    depth = x_buf.shape[2]
    high, low = split(x_buf[slot])
    x3[:, :depth] = high
    x3[:, depth : 2 * depth] = high
    x3[:, 2 * depth :] = low

    @pl.when(step == 0)
    def _():
        pltpu.make_async_copy(z_hbm, z_ref, z_sem).wait()

    out_ref[...] = lax.dot_general(
        z_ref[...], x3[...], (((1,), (1,)), ((), ())), preferred_element_type=jnp.float32
    )


def gram_kernel(lefts, rights, plan, *refs):
    sides = refs[: lefts + len(rights)]
    count = len(plan)
    outs = refs[-2 - count : -2]
    seeds = refs[lefts + len(rights) : -2 - count]
    left3, right3 = refs[-2:]
    rows = sides[0].shape[0]
    slots = [sum(rights[:i]) for i in range(len(rights))]

    @pl.when(pl.program_id(0) == 0)
    def _():
        for index, out in enumerate(outs):
            out[...] = seeds[index][...] if seeds else jnp.zeros_like(out)

    for index in range(lefts):
        width = sides[index].shape[1]
        high, low = split(sides[index][...])
        at = pl.ds(index * width, width)
        left3[:rows, at] = high
        left3[rows : 2 * rows, at] = low
        left3[2 * rows :, at] = high
    for index, fresh in enumerate(rights):
        if not fresh:
            continue
        value = sides[lefts + index][...]
        if index + 1 < len(rights) and not rights[index + 1]:
            value = value + sides[lefts + index + 1][...]
        width = value.shape[1]
        high, low = split(value)
        at = pl.ds(slots[index] * width, width)
        right3[:rows, at] = high
        right3[rows : 2 * rows, at] = high
        right3[2 * rows :, at] = low
    for out, (row, col) in zip(outs, plan):
        high, wide = out.shape
        out[...] += lax.dot_general(
            left3[:, row : row + high],
            right3[:, col : col + wide],
            (((0,), (0,)), ((), ())),
            preferred_element_type=jnp.float32,
        )


def gram_chunk(index, height, lefts, rights, fresh, plan, shapes, seeds):
    width = lefts[0].shape[1]
    steps = height // tile
    first = index * steps
    whole = pl.BlockSpec((tile, width), lambda i: (first + i, 0))
    part = pl.BlockSpec((tile, width), lambda i: (i, 0))
    specs = [part if v.shape[0] == height else whole for v in (*lefts, *rights)]
    fixed = [pl.BlockSpec(s, lambda i: (0, 0)) for s in shapes]
    work = sum(s[0] * s[1] for s in shapes)
    operands = [*lefts, *rights]
    if seeds is not None:
        operands += seeds
        specs += fixed
    return pl.pallas_call(
        functools.partial(gram_kernel, len(lefts), fresh, plan),
        grid=(steps,),
        in_specs=specs,
        out_specs=fixed,
        out_shape=[jax.ShapeDtypeStruct(s, jnp.float32) for s in shapes],
        scratch_shapes=[
            pltpu.VMEM((3 * tile, len(lefts) * width), jnp.bfloat16),
            pltpu.VMEM((3 * tile, sum(fresh) * width), jnp.bfloat16),
        ],
        compiler_params=pltpu.CompilerParams(vmem_limit_bytes=32 * 2**20),
        cost_estimate=pl.CostEstimate(
            flops=6 * work * height,
            bytes_accessed=4 * len(operands) * height * width,
            transcendentals=0,
        ),
        name="gram_chunk",
    )(*operands)


def final_chunk(index, z3, own, groups, previous, columns):
    rows = z3.shape[0]
    width = own.shape[1]
    pieces = z3.shape[1] // (3 * width)
    lists = [v for group in groups for v in group]
    first_row = index * lists[0].shape[0]
    steps = len(groups) * (lists[0].shape[0] // final_tile)
    anywhere = pl.BlockSpec(memory_space=pl.ANY)
    operands = [z3, own, *lists]
    specs = [anywhere] * len(operands)
    aliases = {}
    if previous is not None:
        aliases = {len(operands): 0}
        operands.append(previous)
        specs.append(anywhere)
    first_block = first_row // final_tile
    return pl.pallas_call(
        functools.partial(final_kernel, first_row, pieces, len(groups)),
        grid=(steps,),
        in_specs=specs,
        out_specs=pl.BlockSpec((rows, final_tile), lambda i: (0, first_block + i)),
        out_shape=jax.ShapeDtypeStruct((rows, columns), jnp.float32),
        scratch_shapes=[
            pltpu.VMEM((2, final_tile, pieces * width), jnp.float32),
            pltpu.VMEM((final_tile, 3 * pieces * width), jnp.bfloat16),
            pltpu.VMEM(z3.shape, z3.dtype),
            pltpu.SemaphoreType.DMA(()),
            pltpu.SemaphoreType.DMA((2, pieces)),
        ],
        input_output_aliases=aliases,
        compiler_params=pltpu.CompilerParams(vmem_limit_bytes=40 * 2**20),
        cost_estimate=pl.CostEstimate(
            flops=2 * rows * z3.shape[1] * steps * final_tile,
            bytes_accessed=4 * steps * final_tile * (rows + pieces * width),
            transcendentals=0,
        ),
        name="final_chunk",
    )(*operands)


MESH = pl.DeviceIdType.MESH


def send(source, target, send_sem, recv_sem, device):
    return pltpu.make_async_remote_copy(
        src_ref=source,
        dst_ref=target,
        send_sem=send_sem,
        recv_sem=recv_sem,
        device_id=device,
        device_id_type=MESH,
    )


def greet(device):
    pl.semaphore_signal(pltpu.get_barrier_semaphore(), inc=1, device_id=device, device_id_type=MESH)


def order_kernel(count, position, *refs):
    blocks = refs[:count]
    high_ref, low_ref, buf, stage, sems = refs[count:]
    step = pl.program_id(0)
    share = blocks[0].shape[0]
    rows = stage.shape[0]

    @pl.when(step == 0)
    def _():
        copies = [
            pltpu.make_async_copy(blocks[k], buf.at[pl.ds(k * share, share), :], sems.at[k])
            for k in range(count)
        ]
        for copy in copies:
            copy.start()
        for copy in copies:
            copy.wait()

    def body(index, carry):
        base = index * 8
        for k in range(8):
            stage[pl.ds(base + k, 1), :] = buf[pl.ds(position[step * rows + base + k], 1), :]
        return carry

    lax.fori_loop(0, rows // 8, body, 0)
    high, low = split(stage[...])
    high_ref[0] = high
    low_ref[0] = low


def order(position, blocks):
    share, modes = blocks[0].shape
    count = len(blocks)
    rows = 512
    steps = count * share // rows
    shape = jax.ShapeDtypeStruct((steps, rows, modes), jnp.bfloat16)
    spec = pl.BlockSpec((1, rows, modes), lambda i, p: (i, 0, 0))
    return pl.pallas_call(
        functools.partial(order_kernel, count),
        grid_spec=pltpu.PrefetchScalarGridSpec(
            num_scalar_prefetch=1,
            grid=(steps,),
            in_specs=[pl.BlockSpec(memory_space=pl.ANY)] * count,
            out_specs=[spec, spec],
            scratch_shapes=[
                pltpu.VMEM((count * share, modes), jnp.float32),
                pltpu.VMEM((rows, modes), jnp.float32),
                pltpu.SemaphoreType.DMA((count,)),
            ],
        ),
        out_shape=[shape, shape],
        compiler_params=pltpu.CompilerParams(vmem_limit_bytes=32 * 2**20),
        cost_estimate=pl.CostEstimate(
            flops=0, bytes_accessed=8 * count * share * modes, transcendentals=0
        ),
        name="order",
    )(position, *blocks)


def chain_kernel(
    chips, gram, high_table, low_table, eigen_j, eigen_i, ids_j, ids_i, slope_j, mine,
    met, total, came, w_high, w_low, zt, got, land,
    w_sems, met_send, met_recv, came_send, came_recv, z_send, z_recv,
):
    me = lax.axis_index("harm")
    layer = lax.axis_index("mode")
    core = lax.rem(me, 2)
    chip = lax.div(me, 2)
    partner = me + 1 - 2 * core
    middle = (layer == 1) | (layer == 2)
    span = met.shape[1]
    tiles, rows = w_high.shape[:2]
    peer = 3 - layer
    end = jnp.where(layer == 1, 0, 3)
    keep = jnp.where(layer == 1, 0, 2)
    slot = jnp.where(layer == 1, 0, 1)

    @pl.when(middle)
    def _():
        greet({"harm": partner})
        for d in range(1, chips):
            greet({"harm": lax.rem(chip + d, chips) * 2 + core})
        greet({"mode": layer - 1})
        greet({"mode": layer + 1})
        pl.semaphore_wait(pltpu.get_barrier_semaphore(), chips + 2)
        first = [
            send(
                gram.at[pl.ds((2 * q + 1 - core) * span, span), :],
                met.at[q],
                met_send.at[q],
                met_recv.at[q],
                {"harm": partner},
            )
            for q in range(chips)
        ]
        for copy in first:
            copy.start()
        loads = [
            pltpu.make_async_copy(high_table, w_high, w_sems.at[0]),
            pltpu.make_async_copy(low_table, w_low, w_sems.at[1]),
        ]
        for load in loads:
            load.start()
        for q in range(chips):
            first[q].wait()
            total[q] = gram[pl.ds((2 * q + core) * span, span), :] + met[q]
        second = []
        for d in range(1, chips):
            q = lax.rem(chip + d, chips)
            second.append(
                send(
                    total.at[q],
                    came.at[d - 1],
                    came_send.at[d - 1],
                    came_recv.at[d - 1],
                    {"harm": q * 2 + core},
                )
            )
            second[-1].start()
        for load in loads:
            load.wait()
        for copy in second:
            copy.wait()
        value = total[chip]
        for d in range(1, chips):
            value = value + came[d - 1]
        differ = eigen_j[...] - eigen_i[...]
        value = value * (differ / (differ * differ + regular))
        value = value + jnp.where(ids_j[...] == ids_i[...], slope_j[...], 0.0)
        high, low = split(value)
        both = jnp.concatenate([high, low], axis=0)
        per = zt.shape[2] // rows
        nt = (((1,), (1,)), ((), ()))

        def mix(t, carry):
            part = lax.dot_general(both, w_high[t], nt, preferred_element_type=jnp.float32)
            rest = lax.dot_general(high, w_low[t], nt, preferred_element_type=jnp.float32)
            zt[t // per, :, pl.ds(pl.multiple_of(lax.rem(t, per) * rows, rows), rows)] = (
                part[:span] + part[span:] + rest
            )
            return carry

        lax.fori_loop(0, tiles, mix, 0)
        swap = send(zt.at[pl.ds(2 - keep, 2)], got, z_send.at[0], z_recv.at[0], {"mode": peer})
        swap.start()
        out = send(zt.at[end], land.at[slot], z_send.at[1], z_recv.at[1], {"mode": end})
        out.start()
        mine[slot] = zt[layer]
        swap.wait()
        pass_on = send(
            got.at[end - keep], land.at[1 - slot], z_send.at[2], z_recv.at[2], {"mode": end}
        )
        pass_on.start()
        mine[1 - slot] = got[layer - keep]
        out.wait_send()
        pass_on.wait_send()

    @pl.when(jnp.logical_not(middle))
    def _():
        inward = jnp.where(layer == 0, 1, 2)
        side = jnp.where(layer == 0, 0, 1)
        greet({"mode": inward})
        pl.semaphore_wait(pltpu.get_barrier_semaphore(), 1)
        send(zt.at[0], land.at[side], z_send.at[1], z_recv.at[1], {"mode": inward}).wait_recv()
        send(zt.at[0], land.at[1 - side], z_send.at[2], z_recv.at[2], {"mode": inward}).wait_recv()
        mine[...] = land[...]


def chain(gram, high_table, low_table, eigen_j, eigen_i, ids_j, ids_i, slope_j, harm_count, mode_count):
    chips = harm_count // 2
    span = gram.shape[0] // harm_count
    modes = gram.shape[1]
    rows = high_table.shape[0] * high_table.shape[1] // mode_count
    vmem = pl.BlockSpec(memory_space=pltpu.VMEM)
    return pl.pallas_call(
        functools.partial(chain_kernel, chips),
        in_specs=[vmem] + [pl.BlockSpec(memory_space=pl.ANY)] * 2 + [vmem] * 5,
        out_specs=vmem,
        out_shape=jax.ShapeDtypeStruct((2, span, rows), jnp.float32),
        scratch_shapes=[
            pltpu.VMEM((chips, span, modes), jnp.float32),
            pltpu.VMEM((chips, span, modes), jnp.float32),
            pltpu.VMEM((chips - 1, span, modes), jnp.float32),
            pltpu.VMEM(high_table.shape, jnp.bfloat16),
            pltpu.VMEM(low_table.shape, jnp.bfloat16),
            pltpu.VMEM((mode_count, span, rows), jnp.float32),
            pltpu.VMEM((2, span, rows), jnp.float32),
            pltpu.VMEM((2, span, rows), jnp.float32),
            pltpu.SemaphoreType.DMA((2,)),
            pltpu.SemaphoreType.DMA((chips,)),
            pltpu.SemaphoreType.DMA((chips,)),
            pltpu.SemaphoreType.DMA((chips - 1,)),
            pltpu.SemaphoreType.DMA((chips - 1,)),
            pltpu.SemaphoreType.DMA((3,)),
            pltpu.SemaphoreType.DMA((3,)),
        ],
        compiler_params=pltpu.CompilerParams(
            collective_id=1, has_side_effects=True, vmem_limit_bytes=52 * 2**20
        ),
        name="chain",
    )(gram, high_table, low_table, eigen_j, eigen_i, ids_j, ids_i, slope_j)


def spread_kernel(width, mine, z_ref, land, sends, recvs):
    me = lax.axis_index("harm")
    core = lax.rem(me, 2)
    chip = lax.div(me, 2)
    partner = me + 1 - 2 * core
    across = [chip + 1 - 2 * lax.rem(chip, 2), chip + 2 - 4 * lax.div(chip, 2)]
    opposite = 3 - chip
    greet({"harm": partner})
    for q in across:
        greet({"harm": q * 2 + core})
    pl.semaphore_wait(pltpu.get_barrier_semaphore(), 3)

    def push(source, origin, at, index, device):
        copy = send(source, land.at[origin, at], sends.at[index], recvs.at[index], {"harm": device})
        copy.start()
        return copy

    direct = [push(mine, chip, core, k, across[k] * 2 + core) for k in range(2)]
    pair = [push(mine, chip, core, 2, partner)]
    land[chip, core] = mine[...]
    relay = []
    for k in range(2):
        direct[k].wait()
        origin = across[k]
        relay.append(
            send(
                land.at[origin, core, k],
                land.at[origin, core, k],
                sends.at[3 + k],
                recvs.at[3 + k],
                {"harm": across[1 - k] * 2 + core},
            )
        )
        relay[k].start()
        pair.append(push(land.at[origin, core], origin, core, 5 + k, partner))
    for k in range(2):
        relay[k].wait()
    pair.append(push(land.at[opposite, core], opposite, core, 7, partner))
    for copy in pair:
        copy.wait()
    depth = z_ref.shape[1] // 3
    for q in range(4):
        for side in range(2):
            piece = 1 - q // 2 if side == 0 else 2 + q // 2
            block = jnp.concatenate([land[q, 0, side], land[q, 1, side]], axis=0).T
            high, low = split(block)
            size = block.shape[1]
            at = piece * width + (q % 2) * size
            z_ref[:, at : at + size] = high
            z_ref[:, depth + at : depth + at + size] = low
            z_ref[:, 2 * depth + at : 2 * depth + at + size] = high


def spread(mine, mode_count, width):
    vmem = pl.BlockSpec(memory_space=pltpu.VMEM)
    return pl.pallas_call(
        functools.partial(spread_kernel, width),
        in_specs=[vmem],
        out_specs=vmem,
        out_shape=jax.ShapeDtypeStruct((mine.shape[2], 3 * mode_count * width), jnp.bfloat16),
        scratch_shapes=[
            pltpu.VMEM((4, 2, *mine.shape), jnp.float32),
            pltpu.SemaphoreType.DMA((8,)),
            pltpu.SemaphoreType.DMA((8,)),
        ],
        compiler_params=pltpu.CompilerParams(
            collective_id=2, has_side_effects=True, vmem_limit_bytes=40 * 2**20
        ),
        name="spread",
    )(mine)


def slab_order(slab_rows, row_count, harm_count, harm_index):
    total = slab_rows.shape[0]
    share = total // harm_count
    owner = slab_rows // row_count
    ids = lax.broadcasted_iota(jnp.int32, (harm_count, total), 0)
    hit = (owner[None, :] == ids).astype(jnp.int32)
    running = jnp.cumsum(hit, axis=1)
    rank = jnp.sum(hit * running, axis=0) - 1
    position = (owner ^ harm_index) * share + rank
    slots = lax.broadcasted_iota(jnp.int32, (share, total), 0)
    mine = position[None, :] == slots
    offsets = jnp.sum(jnp.where(mine, (slab_rows - harm_index * row_count)[None, :], 0), axis=1)
    return position, offsets


def line_body(mode_vectors, weights, cotangent, eigenvalues, eigen_cotangent, slab_rows, harm_count, mode_count):
    harm = lax.axis_index("harm")
    layer = lax.axis_index("mode")
    height, width = mode_vectors.shape
    lower = layer <= 1
    part = height // chunks
    own = [mode_vectors[:part]]
    rest, first = lax.optimization_barrier((mode_vectors, own[0]))
    own = [first] + [rest[c * part : (c + 1) * part] for c in range(1, chunks)]
    slope = jnp.split(cotangent, chunks, 0)

    def hop(values, pairs):
        results = []
        for value in values:
            results.append(shift(value, pairs))
        return results

    b1 = hop(own, [(0, 1), (1, 2), (2, 3)])
    a1 = hop(own, [(1, 0), (2, 1), (3, 2)])

    position, offsets = slab_order(slab_rows, height, harm_count, harm)
    picked = jnp.take(weights, offsets, axis=0, mode="clip")
    w_b1 = shift(picked, [(0, 1), (1, 2)])
    w_a1 = shift(picked, [(3, 2), (2, 1)])
    w_third = shift(w_b1, [(1, 2)]) + shift(w_a1, [(2, 1)])
    w_all = jnp.concatenate([picked, w_b1, w_a1, w_third], axis=1)
    pairs = lambda flip: [(n, n ^ flip) for n in range(harm_count)]
    blocks = [w_all] + [lax.ppermute(w_all, "harm", pairs(2 * d)) for d in (1, 2, 3)]
    blocks = [v for block in blocks for v in (block, lax.ppermute(block, "harm", pairs(1)))]
    w_high, w_low = order(position, blocks)

    b2 = hop(b1, [(1, 2), (2, 3)])
    a2 = hop(a1, [(2, 1), (1, 0)])
    edge = hop(slope, [(0, 1), (3, 2)])
    b3 = hop(b2, [(2, 3)])
    a3 = hop(a2, [(1, 0)])

    near = None
    for c in range(chunks):
        near = gram_chunk(
            c, part, [cotangent], [mode_vectors, b1[c], a1[c]], (1, 1, 1),
            ((0, 0),), ((width, 3 * width),), near,
        )
    far_parts = None
    for c in range(chunks):
        side = edge[c]
        if c == 1:
            side, w_high, w_low = lax.optimization_barrier((side, w_high, w_low))
        far_parts = gram_chunk(
            c, part, [cotangent, side], [mode_vectors, b1[c], a1[c], b2[c], a2[c]], (1, 1, 1, 1, 0),
            ((0, 3 * width), (width, 0)), ((width, width), (width, 4 * width)), far_parts,
        )
    top = jnp.concatenate([near[0], far_parts[0]], axis=1)
    gram = jnp.concatenate([top, far_parts[1]], axis=0)

    span = 2 * width // harm_count
    half = harm_count // 2
    last = mode_count - 1
    end = jnp.where(lower, 0, last)
    far = jnp.where(lower, last, 0)
    first_col = jnp.where(harm < half, layer * width + harm * span, end * width + (harm - half) * span)
    blocks = [layer, jnp.maximum(layer - 1, 0), jnp.minimum(layer + 1, last), far]
    row_ids = jnp.concatenate([b * width + jnp.arange(width, dtype=jnp.int32) for b in blocks])
    eigen_i = jnp.concatenate([lax.dynamic_slice_in_dim(eigenvalues, b * width, width) for b in blocks])
    eigen_j = lax.dynamic_slice_in_dim(eigenvalues, first_col, span)
    slope_j = lax.dynamic_slice_in_dim(eigen_cotangent, first_col, span)
    col_ids = first_col + jnp.arange(span, dtype=jnp.int32)
    mine = chain(
        gram, w_high, w_low, eigen_j[:, None], eigen_i[None, :], col_ids[:, None], row_ids[None, :],
        slope_j[:, None], harm_count, mode_count,
    )
    z3 = spread(mine, mode_count, width)

    out = None
    lists = list(zip(b1, b2, b3, a1, a2, a3))
    for first, count in ((0, chunks - 1), (chunks - 1, 1)):
        out = final_chunk(first, z3, mode_vectors, lists[first : first + count], out, height)
    return out


def line(*operands):
    return line_body(*operands)


def solution(mesh):
    harm_count = mesh.shape["harm"]
    mode_count = mesh.shape["mode"]
    placed = (P("harm", "mode"), P("harm", "mode"), P("harm", "mode"), P(), P(), P())
    lined = mode_count == 4 and harm_count == 8
    form = line if lined else plain

    def local(*operands):
        return form(*operands, harm_count, mode_count)

    return jax.shard_map(
        local, mesh=mesh, in_specs=placed, out_specs=P("mode", "harm"), check_vma=False
    )
```
